32 devices in a mesh: gy: 8 (over y, x, core), gz: 4 (over z).
Axes of the slice: x: 2, y: 2, z: 4, core: 2. Of those that a mesh axis runs over, the one named last changes fastest.
Arguments:
- magnetic: float32 [3, 192, 32, 256], P(None, 'gy', 'gz'), may hold values from -6 to 6
- velocity: float32 [3, 192, 32, 256], P(None, 'gy', 'gz'), may hold values from -6 to 6
- diffusivity: float32 [192, 32, 256], P('gy', 'gz'), may hold values from 0.5 to 2
- material: int32 [192, 32, 256], P('gy', 'gz'), may hold values 0 or 1
- plane_rate: float32 [32], P('gz'), may hold values from 0.5 to 2000
- cotangent: float32 [3, 192, 32, 256], P(None, 'gy', 'gz'), may hold values from -6 to 6
Outputs:
- new_field: float32 [3, 192, 32, 256], P(None, 'gy', 'gz')
- adjoint_field: float32 [3, 192, 32, 256], P(None, 'gy', 'gz')
The draws below stay inside these ranges and needn't reach their ends.
Inputs may be any that keep to these rules, and one draw needn't show every extreme that they name: `material`: 1 marks impeller iron.
All inputs are finite; a program needn't handle non-finite values. No bound on the sum of `material` on one device may be relied on, other than what follows from the above.
Results may differ from the reference program's by a relative error of at most 0.000098.
Values sent between devices are 32-bit elements; how exact they have to be, the bound alone decides.
A program may use at most 64 MiB of HBM per device.

```python
import math
import jax
import jax.numpy as jnp
from jax import lax

CY = 24
NX = 256
NY = 192
NZ = 32


def place_ends(array, own_key, least, high):
    index_at = [jax.random.randint(jax.random.fold_in(own_key, axis), (), 0, length) for axis, length in enumerate(array.shape)]
    widest = array.shape.index(max(array.shape))
    beside = index_at[:widest] + [(index_at[widest] + 1) % array.shape[widest]] + index_at[widest + 1:]
    return array.at[tuple(index_at)].set(least).at[tuple(beside)].set(high)


def level_of(key, extent, cuts, low, top_value):
    level = 1.0
    for dim, blocks in cuts:
        heights = jax.random.uniform(jax.random.fold_in(jax.random.fold_in(key, 6), dim), (blocks,), jnp.float32, low / len(cuts), top_value / len(cuts))
        level = level * jnp.repeat(jnp.exp(heights), extent[dim] // blocks).reshape((-1,) + (1,) * (len(extent) - 1 - dim))
    return level


def noise(key, dims, width, most, cuts=(), kind=jnp.bfloat16):
    loudness = level_of(key, dims, cuts, -0.22, 0.18) if cuts else 1.0
    values = jax.random.normal(key, dims, jnp.float32) * width * loudness
    return jnp.minimum(jnp.maximum(values, -most), most).astype(kind)


def setup_inputs(seed: int = 0) -> dict:
    arg_keys = jax.random.split(jax.random.key(seed), 7)
    magnetic = noise(arg_keys[0], (3, NY, NZ, NX), 1.0, 6.0, ((1, 8), (2, 4)), jnp.float32)
    velocity = noise(arg_keys[1], (3, NY, NZ, NX), 1.0, 6.0, ((1, 8), (2, 4)), jnp.float32)
    diffusivity = jnp.clip(jnp.exp(math.log(2.0) - 1.3862944 * jax.random.uniform(arg_keys[2], (NY, NZ, NX), jnp.float32) ** level_of(arg_keys[2], (NY, NZ, NX), ((0, 8), (1, 4)), -0.2, 0.2)), 0.5, 2.0)
    material = place_ends((jax.random.randint(arg_keys[3], (NY, NZ, NX), 0, 4) < 1).astype(jnp.int32), jax.random.fold_in(arg_keys[3], 1), 0, 1)
    plane_rate = jnp.clip(jnp.exp(math.log(2000.0) - 8.2940496 * jax.random.uniform(arg_keys[4], (NZ,), jnp.float32) ** level_of(arg_keys[4], (NZ,), ((0, 4),), -0.2, 0.2)), 0.5, 2000.0)
    cotangent = noise(arg_keys[5], (3, NY, NZ, NX), 1.0, 6.0, ((1, 8), (2, 4)), jnp.float32)
    return dict(magnetic=magnetic, velocity=velocity, diffusivity=diffusivity, material=material, plane_rate=plane_rate, cotangent=cotangent)


step_size = 0.1
iron_factor = 0.2

def slope_y(vector):
    return 0.5 * (vector[:, 2:, 1:-1] - vector[:, :-2, 1:-1])

def slope_z(vector):
    return 0.5 * (vector[:, 1:-1, 2:] - vector[:, 1:-1, :-2])

def slope_x(vector):
    inner = vector[:, 1:-1, 1:-1]
    padded = jnp.pad(inner, ((0, 0), (0, 0), (0, 0), (1, 1)))
    return 0.5 * (padded[..., 2:] - padded[..., :-2])

def curl_of(vector):
    along_y = slope_y(vector)
    along_z = slope_z(vector)
    along_x = slope_x(vector)
    return jnp.stack([along_y[2] - along_z[1], along_z[0] - along_x[2], along_x[1] - along_y[0]])

def induction(padded, coefficients):
    inner = padded[:, 1:-1, 1:-1]
    speed = coefficients[:3]
    spread = coefficients[3]
    crossed = jnp.stack([speed[1] * inner[2] - speed[2] * inner[1], speed[2] * inner[0] - speed[0] * inner[2], speed[0] * inner[1] - speed[1] * inner[0]])
    return curl_of(crossed - spread[None] * curl_of(padded))

def line_solve_ref(line_values, plane_rate):
    stacked = jnp.transpose(line_values, (2, 1, 0, 3)).reshape(NZ, NY, 3 * NX)
    rate_grid = plane_rate[:, None] * jnp.ones((1, NY), jnp.float32)
    lower_band = (-rate_grid).at[:, 0].set(0.0)
    upper_band = (-rate_grid).at[:, -1].set(0.0)
    middle = 1.0 + 2.0 * rate_grid
    solved = lax.linalg.tridiagonal_solve(lower_band, middle, upper_band, stacked)
    return jnp.transpose(solved.reshape(NZ, NY, 3, NX), (2, 1, 0, 3))

def reference(magnetic, velocity, diffusivity, material, plane_rate, cotangent):
    spread = diffusivity * (1.0 - (1.0 - iron_factor) * material.astype(jnp.float32))
    coefficients = jnp.concatenate([velocity, spread[None]], axis=0)
    field_pad = jnp.pad(magnetic, ((0, 0), (4, 4), (4, 4), (0, 0)))
    coef_pad = jnp.pad(coefficients, ((0, 0), (3, 3), (3, 3), (0, 0)))
    starts = jnp.arange(NY // CY, dtype=jnp.int32) * CY

    def forward_block(row_start):
        slab_part = lax.dynamic_slice_in_dim(field_pad, row_start + 2, CY + 4, 1)[:, :, 2:-2]
        near_coef = lax.dynamic_slice_in_dim(coef_pad, row_start + 2, CY + 2, 1)[:, :, 2:-2]
        return induction(slab_part, near_coef)
    change = lax.map(forward_block, starts)
    change = jnp.moveaxis(change, 0, 1).reshape(3, NY, NZ, NX)
    advanced = magnetic + step_size * change
    new_field = line_solve_ref(advanced, plane_rate)
    relaxed = line_solve_ref(cotangent, plane_rate)
    weight_pad = jnp.pad(relaxed, ((0, 0), (2, 2), (2, 2), (0, 0)))

    def adjoint_block(row_start):
        near_coef = lax.dynamic_slice_in_dim(coef_pad, row_start, CY + 6, 1)
        seen_weight = lax.dynamic_slice_in_dim(weight_pad, row_start, CY + 4, 1)
        zero_field = jnp.zeros((3, CY + 8, NZ + 8, NX), jnp.float32)
        outcome, pullback = jax.vjp(lambda probe: induction(probe, near_coef), zero_field)
        return pullback(seen_weight)[0][:, 4:-4, 4:-4]
    pulled = lax.map(adjoint_block, starts)
    pulled = jnp.moveaxis(pulled, 0, 1).reshape(3, NY, NZ, NX)
    adjoint_field = relaxed + step_size * pulled
    return (new_field, adjoint_field)
```

```python
import functools
import jax
import jax.numpy as jnp
from jax import lax
from jax.experimental import pallas as pl
from jax.experimental.pallas import tpu as pltpu
from jax.sharding import PartitionSpec as P

step_size = 0.1
iron_factor = 0.2
MESH = pl.DeviceIdType.MESH
Y_PARTS = (0, 2)
Z_PARTS = (0, 1)


def kernel(
    groups, layers, n, mag, vel, dif, mat, rate, cot, new_out, adj_out,
    bE, gE, wE, hE, v, eta, iron, adj, new, zs, zr, ends, m_tab, inv_tab, al_tab, s_tab, den_tab,
    load_sem, out_sem, ys_sem, yr_sem, zs_sem, zr_sem, gs_sem, gr_sem,
):
    me = lax.axis_index("gy")
    lay = lax.axis_index("gz")
    nx = bE.shape[-1]
    nz = bE.shape[-2]

    loads = [
        pltpu.make_async_copy(mag, bE.at[:, pl.ds(1, n)], load_sem.at[0]),
        pltpu.make_async_copy(cot, wE.at[:, pl.ds(1, n)], load_sem.at[1]),
        pltpu.make_async_copy(vel, v, load_sem.at[2]),
        pltpu.make_async_copy(dif, eta, load_sem.at[3]),
        pltpu.make_async_copy(mat, iron, load_sem.at[4]),
    ]
    for load in loads:
        load.start()

    has_left, has_right = me > 0, me < groups - 1
    has_low, has_high = lay > 0, lay < layers - 1

    barrier = pltpu.get_barrier_semaphore()
    for k in range(1, groups):
        pl.semaphore_signal(
            barrier, inc=1, device_id={"gy": lax.rem(me + k, groups), "gz": lay}, device_id_type=MESH
        )

    @pl.when(has_low)
    def _():
        pl.semaphore_signal(barrier, inc=1, device_id={"gy": me, "gz": lay - 1}, device_id_type=MESH)

    @pl.when(has_high)
    def _():
        pl.semaphore_signal(barrier, inc=1, device_id={"gy": me, "gz": lay + 1}, device_id_type=MESH)

    rim = jnp.zeros((nz, nx), jnp.float32)
    for field in (bE, gE, hE):
        for part in Y_PARTS:
            @pl.when(jnp.logical_not(has_left))
            def _():
                field[part, 0] = rim

            @pl.when(jnp.logical_not(has_right))
            def _():
                field[part, n + 1] = rim

    @pl.when(jnp.logical_not(has_low))
    def _():
        zr[:, 0] = jnp.zeros(zr.shape[:1] + zr.shape[2:], jnp.float32)

    @pl.when(jnp.logical_not(has_high))
    def _():
        zr[:, 1] = jnp.zeros(zr.shape[:1] + zr.shape[2:], jnp.float32)

    sub = lax.broadcasted_iota(jnp.int32, (nz, nx), 0)
    lane = lax.broadcasted_iota(jnp.int32, (nz, nx), 1)
    square = (
        lax.broadcasted_iota(jnp.int32, (nz, nz), 0) == lax.broadcasted_iota(jnp.int32, (nz, nz), 1)
    )
    r = jnp.sum(jnp.where(square, jnp.broadcast_to(rate[...], (nz, nz)), 0.0), axis=1, keepdims=True)
    r = jnp.broadcast_to(r, (nz, nx))

    def pivot(k, p):
        inv = 1.0 / (r + p)
        m = r * inv
        m_tab[k] = m
        inv_tab[k] = inv
        return 1.0 + m * p

    lax.fori_loop(0, n, pivot, 1.0 + r)

    def response(k, above):
        here = m_tab[n - 1 - k] * above
        al_tab[k] = here
        return here

    cc = lax.fori_loop(0, n, response, jnp.ones((nz, nx), jnp.float32))
    aa = m_tab[n - 1]

    def reach(k, s):
        s_tab[k] = s
        den = cc / (1.0 - s * aa)
        den_tab[k] = den
        return aa + cc * s * den

    lax.fori_loop(0, groups, reach, jnp.zeros((nz, nx), jnp.float32))

    def local_solve(field, offset, slot):
        def down(k, held):
            m = m_tab[jnp.maximum(k - 1, 0)]
            rows = tuple(field[c, offset + k] + m * held[c] for c in range(3))
            for c in range(3):
                field[c, offset + k] = rows[c]
            return rows

        zero = jnp.zeros((nz, nx), jnp.float32)
        lax.fori_loop(0, n, down, (zero, zero, zero), unroll=True)

        def up(step, held):
            k = n - 1 - step
            m, inv = m_tab[k], inv_tab[k]
            rows = tuple(field[c, offset + k] * inv + m * held[c] for c in range(3))
            for c in range(3):
                field[c, offset + k] = rows[c]
            return rows

        lax.fori_loop(0, n, up, (zero, zero, zero), unroll=True)
        for c in range(3):
            ends[slot, me, 0, c] = field[c, offset]
            ends[slot, me, 1, c] = field[c, offset + n - 1]

    def gather(slot):
        return [
            pltpu.make_async_remote_copy(
                src_ref=ends.at[slot, me], dst_ref=ends.at[slot, me],
                send_sem=gs_sem.at[slot, k], recv_sem=gr_sem.at[slot, k],
                device_id={"gy": lax.rem(me + k, groups), "gz": lay}, device_id_type=MESH,
            )
            for k in range(1, groups)
        ]

    def gather_wait(slot):
        for k in range(1, groups):
            src = lax.rem(me + groups - k, groups)
            pltpu.make_async_remote_copy(
                src_ref=ends.at[slot, src], dst_ref=ends.at[slot, src],
                send_sem=gs_sem.at[slot, k], recv_sem=gr_sem.at[slot, k],
                device_id={"gy": src, "gz": lay}, device_id_type=MESH,
            ).wait_recv()

    def interface(slot):
        zero = jnp.zeros((nz, nx), jnp.float32)

        def sweep(k, held):
            low, high, s_low, s_high = held
            s, den = s_tab[k], den_tab[k]
            take_low = k < me
            far = groups - 1 - k
            take_high = far > me
            low = tuple(
                jnp.where(take_low, ends[slot, k, 1, c] + den * (low[c] + s * ends[slot, k, 0, c]), low[c])
                for c in range(3)
            )
            high = tuple(
                jnp.where(take_high, ends[slot, far, 0, c] + den * (high[c] + s * ends[slot, far, 1, c]), high[c])
                for c in range(3)
            )
            after = s_tab[k + 1]
            s_low = jnp.where(take_low, after, s_low)
            s_high = jnp.where(take_high, after, s_high)
            return low, high, s_low, s_high

        zeros = (zero, zero, zero)
        low, high, s_low, s_high = lax.fori_loop(0, groups - 1, sweep, (zeros, zeros, zero, zero))
        left_gap, right_gap = 1.0 - s_low * aa, 1.0 - s_high * aa
        det = 1.0 / (left_gap * right_gap - s_low * s_high * cc * cc)
        lefts, rights = [], []
        for c in range(3):
            x = low[c] + s_low * ends[slot, me, 0, c]
            y = high[c] + s_high * ends[slot, me, 1, c]
            lefts.append((right_gap * x + s_low * cc * y) * det)
            rights.append((left_gap * y + s_high * cc * x) * det)
        return lefts, rights

    def y_copies(field, ex):
        lefts, rights = [], []
        for i, part in enumerate(Y_PARTS):
            lefts.append(pltpu.make_async_remote_copy(
                src_ref=field.at[part, 1], dst_ref=field.at[part, n + 1],
                send_sem=ys_sem.at[ex, 0, i], recv_sem=yr_sem.at[ex, 0, i],
                device_id={"gy": jnp.maximum(me - 1, 0), "gz": lay}, device_id_type=MESH))
            rights.append(pltpu.make_async_remote_copy(
                src_ref=field.at[part, n], dst_ref=field.at[part, 0],
                send_sem=ys_sem.at[ex, 1, i], recv_sem=yr_sem.at[ex, 1, i],
                device_id={"gy": jnp.minimum(me + 1, groups - 1), "gz": lay}, device_id_type=MESH))
        return lefts, rights

    def z_copies(ex):
        low = pltpu.make_async_remote_copy(
            src_ref=zs.at[ex, 0], dst_ref=zr.at[ex, 1],
            send_sem=zs_sem.at[ex, 0], recv_sem=zr_sem.at[ex, 0],
            device_id={"gy": me, "gz": jnp.maximum(lay - 1, 0)}, device_id_type=MESH)
        high = pltpu.make_async_remote_copy(
            src_ref=zs.at[ex, 1], dst_ref=zr.at[ex, 0],
            send_sem=zs_sem.at[ex, 1], recv_sem=zr_sem.at[ex, 1],
            device_id={"gy": me, "gz": jnp.minimum(lay + 1, layers - 1)}, device_id_type=MESH)
        return low, high

    def send_y(field, ex):
        lefts, rights = y_copies(field, ex)

        @pl.when(has_left)
        def _():
            for copy in lefts:
                copy.start()

        @pl.when(has_right)
        def _():
            for copy in rights:
                copy.start()

    def send_z(ex):
        low, high = z_copies(ex)

        @pl.when(has_low)
        def _():
            low.start()

        @pl.when(has_high)
        def _():
            high.start()

    def recv(field, ex):
        low, high = z_copies(ex)
        if field is not None:
            lefts, rights = y_copies(field, ex)

            @pl.when(has_right)
            def _():
                for copy in lefts:
                    copy.wait_recv()

            @pl.when(has_left)
            def _():
                for copy in rights:
                    copy.wait_recv()

        @pl.when(has_high)
        def _():
            low.wait_recv()

        @pl.when(has_low)
        def _():
            high.wait_recv()

    def done_sending(field, ex):
        low, high = z_copies(ex)
        if field is not None:
            lefts, rights = y_copies(field, ex)

            @pl.when(has_left)
            def _():
                for copy in lefts:
                    copy.wait_send()

            @pl.when(has_right)
            def _():
                for copy in rights:
                    copy.wait_send()

        @pl.when(has_low)
        def _():
            low.wait_send()

        @pl.when(has_high)
        def _():
            high.wait_send()

    def stage(ex, y, rows):
        for i in range(2):
            zs[ex, 0, i, pl.ds(y, 1), :] = rows[i][0:1]
            zs[ex, 1, i, pl.ds(y, 1), :] = rows[i][nz - 1:nz]

    def slope_x(f):
        ahead = jnp.where(lane == nx - 1, 0.0, pltpu.roll(f, nx - 1, 1))
        behind = jnp.where(lane == 0, 0.0, pltpu.roll(f, 1, 1))
        return 0.5 * (ahead - behind)

    def slope_z(f, ex, i, y):
        below = jnp.broadcast_to(zr[ex, 0, i, pl.ds(y, 1), :], (nz, nx))
        above = jnp.broadcast_to(zr[ex, 1, i, pl.ds(y, 1), :], (nz, nx))
        ahead = jnp.where(sub == nz - 1, above, pltpu.roll(f, nz - 1, 0))
        behind = jnp.where(sub == 0, below, pltpu.roll(f, 1, 0))
        return 0.5 * (ahead - behind)

    def curl(field, ex, y):
        f = [field[c, y + 1] for c in range(3)]
        dy_x = 0.5 * (field[0, y + 2] - field[0, y])
        dy_z = 0.5 * (field[2, y + 2] - field[2, y])
        return (
            dy_z - slope_z(f[1], ex, 1, y),
            slope_z(f[0], ex, 0, y) - slope_x(f[2]),
            slope_x(f[1]) - dy_x,
        ), f

    def each_row(body, unroll=2):
        def some(step, carry):
            for u in range(unroll):
                body(step * unroll + u)
            return carry

        lax.fori_loop(0, n // unroll, some, 0)

    loads[0].wait()
    each_row(lambda y: stage(0, y, (bE[0, y + 1], bE[1, y + 1])), 4)
    count = groups - 1 + has_low.astype(jnp.int32) + has_high.astype(jnp.int32)
    pl.semaphore_wait(barrier, count)
    send_y(bE, 0)
    send_z(0)

    loads[1].wait()
    local_solve(wE, 1, 0)
    for copy in gather(0):
        copy.start()

    for load in loads[2:]:
        load.wait()
    recv(bE, 0)

    def argument(y):
        spread = eta[y] * (1.0 - (1.0 - iron_factor) * iron[y].astype(jnp.float32))
        eta[y] = spread
        turn, b = curl(bE, 0, y)
        s = [v[c, y] for c in range(3)]
        rows = (
            s[1] * b[2] - s[2] * b[1] - spread * turn[0],
            s[2] * b[0] - s[0] * b[2] - spread * turn[1],
            s[0] * b[1] - s[1] * b[0] - spread * turn[2],
        )
        for c in range(3):
            gE[c, y + 1] = rows[c]
        stage(1, y, rows)

    each_row(argument)
    send_y(gE, 1)
    send_z(1)

    gather_wait(0)
    lefts, rights = interface(0)
    for c in range(3):
        wE[c, 0] = lefts[c]
        wE[c, n + 1] = rights[c]

    def relax(y):
        near, far = al_tab[y], al_tab[n - 1 - y]
        rows = [wE[c, y + 1] + near * wE[c, 0] + far * wE[c, n + 1] for c in range(3)]
        for c in range(3):
            wE[c, y + 1] = rows[c]
        stage(2, y, rows)

    each_row(relax)
    send_z(2)

    recv(gE, 1)

    def advance(y):
        turn, _ = curl(gE, 1, y)
        for c in range(3):
            new[c, y] = bE[c, y + 1] + step_size * turn[c]

    each_row(advance)
    local_solve(new, 0, 1)
    for copy in gather(1):
        copy.start()

    recv(None, 2)

    def pull(y):
        turn, w = curl(wE, 2, y)
        s = [v[c, y] for c in range(3)]
        spread = eta[y]
        adj[0, y] = w[0] + step_size * (turn[1] * s[2] - turn[2] * s[1])
        adj[1, y] = w[1] + step_size * (turn[2] * s[0] - turn[0] * s[2])
        adj[2, y] = w[2] + step_size * (turn[0] * s[1] - turn[1] * s[0])
        rows = [spread * turn[c] for c in range(3)]
        for c in range(3):
            hE[c, y + 1] = rows[c]
        stage(3, y, rows)

    each_row(pull)
    send_y(hE, 3)
    send_z(3)

    gather_wait(1)
    lefts, rights = interface(1)
    for c in range(3):
        gE[c, 0] = lefts[c]
        gE[c, n + 1] = rights[c]

    def finish(y):
        near, far = al_tab[y], al_tab[n - 1 - y]
        for c in range(3):
            new[c, y] = new[c, y] + near * gE[c, 0] + far * gE[c, n + 1]

    each_row(finish)
    new_copy = pltpu.make_async_copy(new, new_out, out_sem.at[0])
    new_copy.start()

    recv(hE, 3)

    def finish_adjoint(y):
        turn, _ = curl(hE, 3, y)
        for c in range(3):
            adj[c, y] = adj[c, y] - step_size * turn[c]

    each_row(finish_adjoint)
    adj_copy = pltpu.make_async_copy(adj, adj_out, out_sem.at[1])
    adj_copy.start()
    done_sending(bE, 0)
    done_sending(gE, 1)
    done_sending(None, 2)
    done_sending(hE, 3)
    for slot in range(2):
        for copy in gather(slot):
            copy.wait_send()
    new_copy.wait()
    adj_copy.wait()


def local(groups, layers, magnetic, velocity, diffusivity, material, plane_rate, cotangent):
    _, n, nz, nx = magnetic.shape
    block = (3, n, nz, nx)
    rimmed = (3, n + 2, nz, nx)
    f32 = jnp.float32
    anywhere = pl.BlockSpec(memory_space=pl.ANY)
    inside = pl.BlockSpec(memory_space=pltpu.VMEM)
    return tuple(pl.pallas_call(
        functools.partial(kernel, groups, layers, n),
        out_shape=[jax.ShapeDtypeStruct(block, f32)] * 2,
        in_specs=[anywhere] * 4 + [inside] + [anywhere],
        out_specs=[anywhere] * 2,
        scratch_shapes=[
            pltpu.VMEM(rimmed, f32),
            pltpu.VMEM(rimmed, f32),
            pltpu.VMEM(rimmed, f32),
            pltpu.VMEM(rimmed, f32),
            pltpu.VMEM(block, f32),
            pltpu.VMEM((n, nz, nx), f32),
            pltpu.VMEM((n, nz, nx), jnp.int32),
            pltpu.VMEM(block, f32),
            pltpu.VMEM(block, f32),
            pltpu.VMEM((4, 2, 2, n, nx), f32),
            pltpu.VMEM((4, 2, 2, n, nx), f32),
            pltpu.VMEM((2, groups, 2, 3, nz, nx), f32),
            pltpu.VMEM((n, nz, nx), f32),
            pltpu.VMEM((n, nz, nx), f32),
            pltpu.VMEM((n, nz, nx), f32),
            pltpu.VMEM((groups, nz, nx), f32),
            pltpu.VMEM((groups, nz, nx), f32),
            pltpu.SemaphoreType.DMA((5,)),
            pltpu.SemaphoreType.DMA((2,)),
            pltpu.SemaphoreType.DMA((4, 2, 2)),
            pltpu.SemaphoreType.DMA((4, 2, 2)),
            pltpu.SemaphoreType.DMA((4, 2)),
            pltpu.SemaphoreType.DMA((4, 2)),
            pltpu.SemaphoreType.DMA((2, groups)),
            pltpu.SemaphoreType.DMA((2, groups)),
        ],
        compiler_params=pltpu.CompilerParams(
            collective_id=0, has_side_effects=True, vmem_limit_bytes=24 * 2**20
        ),
    )(magnetic, velocity, diffusivity, material, plane_rate.reshape(1, nz), cotangent))


def solution(mesh):
    in_specs = (
        P(None, "gy", "gz", None),
        P(None, "gy", "gz", None),
        P("gy", "gz", None),
        P("gy", "gz", None),
        P("gz"),
        P(None, "gy", "gz", None),
    )
    out_specs = (P(None, "gy", "gz", None), P(None, "gy", "gz", None))
    body = functools.partial(local, mesh.shape["gy"], mesh.shape["gz"])
    return jax.shard_map(body, mesh=mesh, in_specs=in_specs, out_specs=out_specs, check_vma=False)
```

```python
import functools
import jax
import jax.numpy as jnp
from jax import lax
from jax.experimental import pallas as pl
from jax.experimental.pallas import tpu as pltpu
from jax.sharding import PartitionSpec as P

step_size = 0.1
iron_factor = 0.2
MESH = pl.DeviceIdType.MESH
Y_PARTS = (0, 2)
Z_PARTS = (0, 1)


def kernel(
    groups, layers, n, mag, vel, dif, mat, rate, cot, new, adj,
    bE, gE, wE, hE, v, eta, iron, rate_row, zs, zr, ends, m_tab, inv_tab, al_tab, s_tab, den_tab,
    load_sem, ys_sem, yr_sem, zs_sem, zr_sem, gs_sem, gr_sem,
):
    me = lax.axis_index("gy")
    lay = lax.axis_index("gz")
    nx = bE.shape[-1]
    nz = bE.shape[-2]

    rate_load = pltpu.make_async_copy(rate, rate_row, load_sem.at[5])
    rate_load.start()
    loads = [
        pltpu.make_async_copy(mag, bE.at[:, pl.ds(1, n)], load_sem.at[0]),
        pltpu.make_async_copy(cot, wE.at[:, pl.ds(1, n)], load_sem.at[1]),
        pltpu.make_async_copy(vel, v, load_sem.at[2]),
        pltpu.make_async_copy(dif, eta, load_sem.at[3]),
        pltpu.make_async_copy(mat, iron, load_sem.at[4]),
    ]
    for load in loads:
        load.start()

    has_left, has_right = me > 0, me < groups - 1
    has_low, has_high = lay > 0, lay < layers - 1

    barrier = pltpu.get_barrier_semaphore()
    for k in range(1, groups):
        pl.semaphore_signal(
            barrier, inc=1, device_id={"gy": lax.rem(me + k, groups), "gz": lay}, device_id_type=MESH
        )

    @pl.when(has_low)
    def _():
        pl.semaphore_signal(barrier, inc=1, device_id={"gy": me, "gz": lay - 1}, device_id_type=MESH)

    @pl.when(has_high)
    def _():
        pl.semaphore_signal(barrier, inc=1, device_id={"gy": me, "gz": lay + 1}, device_id_type=MESH)

    rim = jnp.zeros((nz, nx), jnp.float32)
    for field in (bE, gE, hE):
        for part in Y_PARTS:
            @pl.when(jnp.logical_not(has_left))
            def _():
                field[part, 0] = rim

            @pl.when(jnp.logical_not(has_right))
            def _():
                field[part, n + 1] = rim

    @pl.when(jnp.logical_not(has_low))
    def _():
        zr[:, 0] = jnp.zeros(zr.shape[:1] + zr.shape[2:], jnp.float32)

    @pl.when(jnp.logical_not(has_high))
    def _():
        zr[:, 1] = jnp.zeros(zr.shape[:1] + zr.shape[2:], jnp.float32)

    sub = lax.broadcasted_iota(jnp.int32, (nz, nx), 0)
    lane = lax.broadcasted_iota(jnp.int32, (nz, nx), 1)
    square = (
        lax.broadcasted_iota(jnp.int32, (nz, nz), 0) == lax.broadcasted_iota(jnp.int32, (nz, nz), 1)
    )
    rate_load.wait()
    r = jnp.sum(jnp.where(square, jnp.broadcast_to(rate_row[...], (nz, nz)), 0.0), axis=1, keepdims=True)
    r = jnp.broadcast_to(r, (nz, nx))

    def pivot(k, p):
        inv = 1.0 / (r + p)
        m = r * inv
        m_tab[k] = m
        inv_tab[k] = inv
        return 1.0 + m * p

    lax.fori_loop(0, n, pivot, 1.0 + r)

    def response(k, above):
        here = m_tab[n - 1 - k] * above
        al_tab[k] = here
        return here

    cc = lax.fori_loop(0, n, response, jnp.ones((nz, nx), jnp.float32))
    aa = m_tab[n - 1]

    def reach(k, s):
        s_tab[k] = s
        den = cc / (1.0 - s * aa)
        den_tab[k] = den
        return aa + cc * s * den

    lax.fori_loop(0, groups, reach, jnp.zeros((nz, nx), jnp.float32))

    def local_solve(field, offset, slot):
        def down(k, held):
            m = m_tab[jnp.maximum(k - 1, 0)]
            rows = tuple(field[c, offset + k] + m * held[c] for c in range(3))
            for c in range(3):
                field[c, offset + k] = rows[c]
            return rows

        zero = jnp.zeros((nz, nx), jnp.float32)
        lax.fori_loop(0, n, down, (zero, zero, zero), unroll=True)

        def up(step, held):
            k = n - 1 - step
            m, inv = m_tab[k], inv_tab[k]
            rows = tuple(field[c, offset + k] * inv + m * held[c] for c in range(3))
            for c in range(3):
                field[c, offset + k] = rows[c]
            return rows

        lax.fori_loop(0, n, up, (zero, zero, zero), unroll=True)
        for c in range(3):
            ends[slot, me, 0, c] = field[c, offset]
            ends[slot, me, 1, c] = field[c, offset + n - 1]

    def gather(slot):
        return [
            pltpu.make_async_remote_copy(
                src_ref=ends.at[slot, me], dst_ref=ends.at[slot, me],
                send_sem=gs_sem.at[slot, k], recv_sem=gr_sem.at[slot, k],
                device_id={"gy": lax.rem(me + k, groups), "gz": lay}, device_id_type=MESH,
            )
            for k in range(1, groups)
        ]

    def gather_wait(slot):
        for k in range(1, groups):
            src = lax.rem(me + groups - k, groups)
            pltpu.make_async_remote_copy(
                src_ref=ends.at[slot, src], dst_ref=ends.at[slot, src],
                send_sem=gs_sem.at[slot, k], recv_sem=gr_sem.at[slot, k],
                device_id={"gy": src, "gz": lay}, device_id_type=MESH,
            ).wait_recv()

    def interface(slot):
        zero = jnp.zeros((nz, nx), jnp.float32)

        def sweep(k, held):
            low, high, s_low, s_high = held
            s, den = s_tab[k], den_tab[k]
            take_low = k < me
            far = groups - 1 - k
            take_high = far > me
            low = tuple(
                jnp.where(take_low, ends[slot, k, 1, c] + den * (low[c] + s * ends[slot, k, 0, c]), low[c])
                for c in range(3)
            )
            high = tuple(
                jnp.where(take_high, ends[slot, far, 0, c] + den * (high[c] + s * ends[slot, far, 1, c]), high[c])
                for c in range(3)
            )
            after = s_tab[k + 1]
            s_low = jnp.where(take_low, after, s_low)
            s_high = jnp.where(take_high, after, s_high)
            return low, high, s_low, s_high

        zeros = (zero, zero, zero)
        low, high, s_low, s_high = lax.fori_loop(0, groups - 1, sweep, (zeros, zeros, zero, zero))
        left_gap, right_gap = 1.0 - s_low * aa, 1.0 - s_high * aa
        det = 1.0 / (left_gap * right_gap - s_low * s_high * cc * cc)
        lefts, rights = [], []
        for c in range(3):
            x = low[c] + s_low * ends[slot, me, 0, c]
            y = high[c] + s_high * ends[slot, me, 1, c]
            lefts.append((right_gap * x + s_low * cc * y) * det)
            rights.append((left_gap * y + s_high * cc * x) * det)
        return lefts, rights

    def y_copies(field, ex):
        lefts, rights = [], []
        for i, part in enumerate(Y_PARTS):
            lefts.append(pltpu.make_async_remote_copy(
                src_ref=field.at[part, 1], dst_ref=field.at[part, n + 1],
                send_sem=ys_sem.at[ex, 0, i], recv_sem=yr_sem.at[ex, 0, i],
                device_id={"gy": jnp.maximum(me - 1, 0), "gz": lay}, device_id_type=MESH))
            rights.append(pltpu.make_async_remote_copy(
                src_ref=field.at[part, n], dst_ref=field.at[part, 0],
                send_sem=ys_sem.at[ex, 1, i], recv_sem=yr_sem.at[ex, 1, i],
                device_id={"gy": jnp.minimum(me + 1, groups - 1), "gz": lay}, device_id_type=MESH))
        return lefts, rights

    def z_copies(ex):
        low = pltpu.make_async_remote_copy(
            src_ref=zs.at[ex, 0], dst_ref=zr.at[ex, 1],
            send_sem=zs_sem.at[ex, 0], recv_sem=zr_sem.at[ex, 0],
            device_id={"gy": me, "gz": jnp.maximum(lay - 1, 0)}, device_id_type=MESH)
        high = pltpu.make_async_remote_copy(
            src_ref=zs.at[ex, 1], dst_ref=zr.at[ex, 0],
            send_sem=zs_sem.at[ex, 1], recv_sem=zr_sem.at[ex, 1],
            device_id={"gy": me, "gz": jnp.minimum(lay + 1, layers - 1)}, device_id_type=MESH)
        return low, high

    def send_y(field, ex):
        lefts, rights = y_copies(field, ex)

        @pl.when(has_left)
        def _():
            for copy in lefts:
                copy.start()

        @pl.when(has_right)
        def _():
            for copy in rights:
                copy.start()

    def send_z(ex):
        low, high = z_copies(ex)

        @pl.when(has_low)
        def _():
            low.start()

        @pl.when(has_high)
        def _():
            high.start()

    def recv(field, ex):
        low, high = z_copies(ex)
        if field is not None:
            lefts, rights = y_copies(field, ex)

            @pl.when(has_right)
            def _():
                for copy in lefts:
                    copy.wait_recv()

            @pl.when(has_left)
            def _():
                for copy in rights:
                    copy.wait_recv()

        @pl.when(has_high)
        def _():
            low.wait_recv()

        @pl.when(has_low)
        def _():
            high.wait_recv()

    def done_sending(field, ex):
        low, high = z_copies(ex)
        if field is not None:
            lefts, rights = y_copies(field, ex)

            @pl.when(has_left)
            def _():
                for copy in lefts:
                    copy.wait_send()

            @pl.when(has_right)
            def _():
                for copy in rights:
                    copy.wait_send()

        @pl.when(has_low)
        def _():
            low.wait_send()

        @pl.when(has_high)
        def _():
            high.wait_send()

    def stage(ex, y, rows):
        for i in range(2):
            zs[ex, 0, i, pl.ds(y, 1), :] = rows[i][0:1]
            zs[ex, 1, i, pl.ds(y, 1), :] = rows[i][nz - 1:nz]

    def slope_x(f):
        ahead = jnp.where(lane == nx - 1, 0.0, pltpu.roll(f, nx - 1, 1))
        behind = jnp.where(lane == 0, 0.0, pltpu.roll(f, 1, 1))
        return 0.5 * (ahead - behind)

    def slope_z(f, ex, i, y):
        below = jnp.broadcast_to(zr[ex, 0, i, pl.ds(y, 1), :], (nz, nx))
        above = jnp.broadcast_to(zr[ex, 1, i, pl.ds(y, 1), :], (nz, nx))
        ahead = jnp.where(sub == nz - 1, above, pltpu.roll(f, nz - 1, 0))
        behind = jnp.where(sub == 0, below, pltpu.roll(f, 1, 0))
        return 0.5 * (ahead - behind)

    def curl(field, ex, y):
        f = [field[c, y + 1] for c in range(3)]
        dy_x = 0.5 * (field[0, y + 2] - field[0, y])
        dy_z = 0.5 * (field[2, y + 2] - field[2, y])
        return (
            dy_z - slope_z(f[1], ex, 1, y),
            slope_z(f[0], ex, 0, y) - slope_x(f[2]),
            slope_x(f[1]) - dy_x,
        ), f

    def each_row(body, unroll=2):
        def some(step, carry):
            for u in range(unroll):
                body(step * unroll + u)
            return carry

        lax.fori_loop(0, n // unroll, some, 0)

    loads[0].wait()
    each_row(lambda y: stage(0, y, (bE[0, y + 1], bE[1, y + 1])), 4)
    count = groups - 1 + has_low.astype(jnp.int32) + has_high.astype(jnp.int32)
    pl.semaphore_wait(barrier, count)
    send_y(bE, 0)
    send_z(0)

    loads[1].wait()
    local_solve(wE, 1, 0)
    for copy in gather(0):
        copy.start()

    for load in loads[2:]:
        load.wait()
    recv(bE, 0)

    def argument(y):
        spread = eta[y] * (1.0 - (1.0 - iron_factor) * iron[y].astype(jnp.float32))
        eta[y] = spread
        turn, b = curl(bE, 0, y)
        s = [v[c, y] for c in range(3)]
        rows = (
            s[1] * b[2] - s[2] * b[1] - spread * turn[0],
            s[2] * b[0] - s[0] * b[2] - spread * turn[1],
            s[0] * b[1] - s[1] * b[0] - spread * turn[2],
        )
        for c in range(3):
            gE[c, y + 1] = rows[c]
        stage(1, y, rows)

    each_row(argument)
    send_y(gE, 1)
    send_z(1)

    gather_wait(0)
    lefts, rights = interface(0)
    for c in range(3):
        wE[c, 0] = lefts[c]
        wE[c, n + 1] = rights[c]

    def relax(y):
        near, far = al_tab[y], al_tab[n - 1 - y]
        rows = [wE[c, y + 1] + near * wE[c, 0] + far * wE[c, n + 1] for c in range(3)]
        for c in range(3):
            wE[c, y + 1] = rows[c]
        stage(2, y, rows)

    each_row(relax)
    send_z(2)

    recv(gE, 1)

    def advance(y):
        turn, _ = curl(gE, 1, y)
        for c in range(3):
            new[c, y] = bE[c, y + 1] + step_size * turn[c]

    each_row(advance)
    local_solve(new, 0, 1)
    for copy in gather(1):
        copy.start()

    recv(None, 2)

    def pull(y):
        turn, w = curl(wE, 2, y)
        s = [v[c, y] for c in range(3)]
        spread = eta[y]
        adj[0, y] = w[0] + step_size * (turn[1] * s[2] - turn[2] * s[1])
        adj[1, y] = w[1] + step_size * (turn[2] * s[0] - turn[0] * s[2])
        adj[2, y] = w[2] + step_size * (turn[0] * s[1] - turn[1] * s[0])
        rows = [spread * turn[c] for c in range(3)]
        for c in range(3):
            hE[c, y + 1] = rows[c]
        stage(3, y, rows)

    each_row(pull)
    send_y(hE, 3)
    send_z(3)

    gather_wait(1)
    lefts, rights = interface(1)
    for c in range(3):
        gE[c, 0] = lefts[c]
        gE[c, n + 1] = rights[c]

    def finish(y):
        near, far = al_tab[y], al_tab[n - 1 - y]
        for c in range(3):
            new[c, y] = new[c, y] + near * gE[c, 0] + far * gE[c, n + 1]

    each_row(finish)

    recv(hE, 3)

    def finish_adjoint(y):
        turn, _ = curl(hE, 3, y)
        for c in range(3):
            adj[c, y] = adj[c, y] - step_size * turn[c]

    each_row(finish_adjoint)
    done_sending(bE, 0)
    done_sending(gE, 1)
    done_sending(None, 2)
    done_sending(hE, 3)
    for slot in range(2):
        for copy in gather(slot):
            copy.wait_send()


def hand_over(new, adj, new_out, adj_out, sem):
    copies = [
        pltpu.make_async_copy(new, new_out, sem.at[0]),
        pltpu.make_async_copy(adj, adj_out, sem.at[1]),
    ]
    for copy in copies:
        copy.start()
    for copy in copies:
        copy.wait()


def local(groups, layers, magnetic, velocity, diffusivity, material, plane_rate, cotangent):
    _, n, nz, nx = magnetic.shape
    block = (3, n, nz, nx)
    rimmed = (3, n + 2, nz, nx)
    f32 = jnp.float32
    anywhere = pl.BlockSpec(memory_space=pl.ANY)
    inside = pl.BlockSpec(memory_space=pltpu.VMEM)
    args = [
        pltpu.with_memory_space_constraint(array, pltpu.HBM)
        for array in (magnetic, velocity, diffusivity, material, plane_rate.reshape(1, nz), cotangent)
    ]
    new, adj = pl.pallas_call(
        functools.partial(kernel, groups, layers, n),
        out_shape=[jax.ShapeDtypeStruct(block, f32)] * 2,
        in_specs=[anywhere] * 6,
        out_specs=[inside] * 2,
        scratch_shapes=[
            pltpu.VMEM(rimmed, f32),
            pltpu.VMEM(rimmed, f32),
            pltpu.VMEM(rimmed, f32),
            pltpu.VMEM(rimmed, f32),
            pltpu.VMEM(block, f32),
            pltpu.VMEM((n, nz, nx), f32),
            pltpu.VMEM((n, nz, nx), jnp.int32),
            pltpu.VMEM((1, nz), f32),
            pltpu.VMEM((4, 2, 2, n, nx), f32),
            pltpu.VMEM((4, 2, 2, n, nx), f32),
            pltpu.VMEM((2, groups, 2, 3, nz, nx), f32),
            pltpu.VMEM((n, nz, nx), f32),
            pltpu.VMEM((n, nz, nx), f32),
            pltpu.VMEM((n, nz, nx), f32),
            pltpu.VMEM((groups, nz, nx), f32),
            pltpu.VMEM((groups, nz, nx), f32),
            pltpu.SemaphoreType.DMA((6,)),
            pltpu.SemaphoreType.DMA((4, 2, 2)),
            pltpu.SemaphoreType.DMA((4, 2, 2)),
            pltpu.SemaphoreType.DMA((4, 2)),
            pltpu.SemaphoreType.DMA((4, 2)),
            pltpu.SemaphoreType.DMA((2, groups)),
            pltpu.SemaphoreType.DMA((2, groups)),
        ],
        compiler_params=pltpu.CompilerParams(
            collective_id=0, has_side_effects=True, vmem_limit_bytes=24 * 2**20
        ),
    )(*args)
    return tuple(pl.pallas_call(
        hand_over,
        out_shape=[jax.ShapeDtypeStruct(block, f32)] * 2,
        in_specs=[anywhere] * 2,
        out_specs=[anywhere] * 2,
        scratch_shapes=[pltpu.SemaphoreType.DMA((2,))],
        compiler_params=pltpu.CompilerParams(vmem_limit_bytes=2**20),
    )(new, adj))


def solution(mesh):
    in_specs = (
        P(None, "gy", "gz", None),
        P(None, "gy", "gz", None),
        P("gy", "gz", None),
        P("gy", "gz", None),
        P("gz"),
        P(None, "gy", "gz", None),
    )
    out_specs = (P(None, "gy", "gz", None), P(None, "gy", "gz", None))
    body = functools.partial(local, mesh.shape["gy"], mesh.shape["gz"])
    return jax.shard_map(body, mesh=mesh, in_specs=in_specs, out_specs=out_specs, check_vma=False)
```

```python
import functools
import jax
import jax.numpy as jnp
from jax import lax
from jax.experimental import pallas as pl
from jax.experimental.pallas import tpu as pltpu
from jax.sharding import PartitionSpec as P

step_size = 0.1
iron_factor = 0.2
MESH = pl.DeviceIdType.MESH
Y_PARTS = (0, 2)
Z_PARTS = (0, 1)


def kernel(
    groups, layers, n, mag, vel, dif, mat, rate, cot, new, adj,
    bE, gE, wE, hE, v, eta, iron, rate_row, zs, zr, ends, sums, m_tab, inv_tab, al_tab, s_tab, den_tab, mix,
    load_sem, ys_sem, yr_sem, zs_sem, zr_sem, gs_sem, gr_sem,
):
    me = lax.axis_index("gy")
    lay = lax.axis_index("gz")
    nx = bE.shape[-1]
    nz = bE.shape[-2]
    parts, depth = zs.shape[2], zs.shape[4]

    rate_load = pltpu.make_async_copy(rate, rate_row, load_sem.at[5])
    rate_load.start()
    loads = [
        pltpu.make_async_copy(mag, bE.at[:, pl.ds(1, n)], load_sem.at[0]),
        pltpu.make_async_copy(cot, wE.at[:, pl.ds(1, n)], load_sem.at[1]),
        pltpu.make_async_copy(vel, v, load_sem.at[2]),
        pltpu.make_async_copy(dif, eta, load_sem.at[3]),
        pltpu.make_async_copy(mat, iron, load_sem.at[4]),
    ]
    for load in loads:
        load.start()

    has_left, has_right = me > 0, me < groups - 1
    has_low, has_high = lay > 0, lay < layers - 1

    barrier = pltpu.get_barrier_semaphore()
    for k in range(1, groups):
        pl.semaphore_signal(
            barrier, inc=1, device_id={"gy": lax.rem(me + k, groups), "gz": lay}, device_id_type=MESH
        )

    @pl.when(has_low)
    def _():
        pl.semaphore_signal(barrier, inc=1, device_id={"gy": me, "gz": lay - 1}, device_id_type=MESH)

    @pl.when(has_high)
    def _():
        pl.semaphore_signal(barrier, inc=1, device_id={"gy": me, "gz": lay + 1}, device_id_type=MESH)

    rim = jnp.zeros((nz, nx), jnp.float32)
    for field in (bE, gE, hE):
        for part in Y_PARTS:
            @pl.when(jnp.logical_not(has_left))
            def _():
                field[part, 0] = rim

            @pl.when(jnp.logical_not(has_right))
            def _():
                field[part, n + 1] = rim

    @pl.when(jnp.logical_not(has_low))
    def _():
        zr[:, 0] = jnp.zeros(zr.shape[:1] + zr.shape[2:], jnp.float32)

    @pl.when(jnp.logical_not(has_high))
    def _():
        zr[:, 1] = jnp.zeros(zr.shape[:1] + zr.shape[2:], jnp.float32)

    sub = lax.broadcasted_iota(jnp.int32, (nz, nx), 0)
    lane = lax.broadcasted_iota(jnp.int32, (nz, nx), 1)
    square = (
        lax.broadcasted_iota(jnp.int32, (nz, nz), 0) == lax.broadcasted_iota(jnp.int32, (nz, nz), 1)
    )
    rate_load.wait()
    r = jnp.sum(jnp.where(square, jnp.broadcast_to(rate_row[...], (nz, nz)), 0.0), axis=1, keepdims=True)
    r = jnp.broadcast_to(r, (nz, nx))

    def pivot(k, p):
        inv = 1.0 / (r + p)
        m = r * inv
        m_tab[k] = m
        inv_tab[k] = inv
        return 1.0 + m * p

    lax.fori_loop(0, n, pivot, 1.0 + r)

    def response(k, above):
        here = m_tab[n - 1 - k] * above
        al_tab[k] = here
        return here

    cc = lax.fori_loop(0, n, response, jnp.ones((nz, nx), jnp.float32))
    aa = m_tab[n - 1]

    def reach(k, s):
        s_tab[k] = s
        den = cc / (1.0 - s * aa)
        den_tab[k] = den
        return aa + cc * s * den

    lax.fori_loop(0, groups, reach, jnp.zeros((nz, nx), jnp.float32))
    s_low, s_high = s_tab[me], s_tab[groups - 1 - me]
    left_gap, right_gap = 1.0 - s_low * aa, 1.0 - s_high * aa
    det = 1.0 / (left_gap * right_gap - s_low * s_high * cc * cc)
    mix[0] = right_gap * det
    mix[1] = s_low * cc * det
    mix[2] = left_gap * det
    mix[3] = s_high * cc * det
    mix[4] = den_tab[me] * s_low
    mix[5] = den_tab[groups - 1 - me] * s_high
    mix[6] = s_low
    mix[7] = s_high

    def local_solve(field, offset, slot):
        def down(k, held):
            m = m_tab[jnp.maximum(k - 1, 0)]
            rows = tuple(field[c, offset + k] + m * held[c] for c in range(3))
            for c in range(3):
                field[c, offset + k] = rows[c]
            return rows

        zero = jnp.zeros((nz, nx), jnp.float32)
        lax.fori_loop(0, n, down, (zero, zero, zero), unroll=True)

        def up(step, held):
            k = n - 1 - step
            m, inv = m_tab[k], inv_tab[k]
            rows = tuple(field[c, offset + k] * inv + m * held[c] for c in range(3))
            for c in range(3):
                field[c, offset + k] = rows[c]
            return rows

        lax.fori_loop(0, n, up, (zero, zero, zero), unroll=True)
        for c in range(3):
            first, last = field[c, offset], field[c, offset + n - 1]
            sums[slot, 0, c] = last + mix[4] * first
            sums[slot, 1, c] = first + mix[5] * last

    def gather(slot):
        copies = []
        for k in range(1, groups):
            partner = lax.rem(me + k, groups)
            copies.append(pltpu.make_async_remote_copy(
                src_ref=sums.at[slot, (partner < me).astype(jnp.int32)], dst_ref=ends.at[slot, me],
                send_sem=gs_sem.at[slot, k], recv_sem=gr_sem.at[slot, k],
                device_id={"gy": partner, "gz": lay}, device_id_type=MESH,
            ))
        return copies

    def gather_wait(slot):
        for k in range(1, groups):
            src = lax.rem(me + groups - k, groups)
            pltpu.make_async_remote_copy(
                src_ref=ends.at[slot, src], dst_ref=ends.at[slot, src],
                send_sem=gs_sem.at[slot, k], recv_sem=gr_sem.at[slot, k],
                device_id={"gy": src, "gz": lay}, device_id_type=MESH,
            ).wait_recv()

    def interface(slot, field, offset):
        zero = jnp.zeros((nz, nx), jnp.float32)

        def sweep(k, held):
            low, high = held
            den = den_tab[k]
            far = groups - 1 - k
            low = tuple(jnp.where(k < me, ends[slot, k, c] + den * low[c], low[c]) for c in range(3))
            high = tuple(jnp.where(far > me, ends[slot, far, c] + den * high[c], high[c]) for c in range(3))
            return low, high

        zeros = (zero, zero, zero)
        low, high = lax.fori_loop(0, groups - 1, sweep, (zeros, zeros), unroll=groups <= 8)
        lefts, rights = [], []
        for c in range(3):
            x = low[c] + mix[6] * field[c, offset]
            y = high[c] + mix[7] * field[c, offset + n - 1]
            lefts.append(mix[0] * x + mix[1] * y)
            rights.append(mix[2] * y + mix[3] * x)
        return lefts, rights

    def y_copies(field, ex):
        lefts, rights = [], []
        for i, part in enumerate(Y_PARTS):
            lefts.append(pltpu.make_async_remote_copy(
                src_ref=field.at[part, 1], dst_ref=field.at[part, n + 1],
                send_sem=ys_sem.at[ex, 0, i], recv_sem=yr_sem.at[ex, 0, i],
                device_id={"gy": jnp.maximum(me - 1, 0), "gz": lay}, device_id_type=MESH))
            rights.append(pltpu.make_async_remote_copy(
                src_ref=field.at[part, n], dst_ref=field.at[part, 0],
                send_sem=ys_sem.at[ex, 1, i], recv_sem=yr_sem.at[ex, 1, i],
                device_id={"gy": jnp.minimum(me + 1, groups - 1), "gz": lay}, device_id_type=MESH))
        return lefts, rights

    def z_copies(ex, part):
        low = pltpu.make_async_remote_copy(
            src_ref=zs.at[ex, 0, part], dst_ref=zr.at[ex, 1, part],
            send_sem=zs_sem.at[ex, 0, part], recv_sem=zr_sem.at[ex, 0, part],
            device_id={"gy": me, "gz": jnp.maximum(lay - 1, 0)}, device_id_type=MESH)
        high = pltpu.make_async_remote_copy(
            src_ref=zs.at[ex, 1, part], dst_ref=zr.at[ex, 0, part],
            send_sem=zs_sem.at[ex, 1, part], recv_sem=zr_sem.at[ex, 1, part],
            device_id={"gy": me, "gz": jnp.minimum(lay + 1, layers - 1)}, device_id_type=MESH)
        return low, high

    def send_left(field, ex):
        @pl.when(has_left)
        def _():
            for copy in y_copies(field, ex)[0]:
                copy.start()

    def send_right(field, ex):
        @pl.when(has_right)
        def _():
            for copy in y_copies(field, ex)[1]:
                copy.start()

    def send_z(ex, part):
        low, high = z_copies(ex, part)

        @pl.when(has_low)
        def _():
            low.start()

        @pl.when(has_high)
        def _():
            high.start()

    def recv_left(field, ex):
        @pl.when(has_left)
        def _():
            for copy in y_copies(field, ex)[1]:
                copy.wait_recv()

    def recv_right(field, ex):
        @pl.when(has_right)
        def _():
            for copy in y_copies(field, ex)[0]:
                copy.wait_recv()

    def recv_z(ex, part):
        low, high = z_copies(ex, part)

        @pl.when(has_high)
        def _():
            low.wait_recv()

        @pl.when(has_low)
        def _():
            high.wait_recv()

    def done_sending(field, ex):
        if field is not None:
            lefts, rights = y_copies(field, ex)

            @pl.when(has_left)
            def _():
                for copy in lefts:
                    copy.wait_send()

            @pl.when(has_right)
            def _():
                for copy in rights:
                    copy.wait_send()

        for part in range(parts):
            low, high = z_copies(ex, part)

            @pl.when(has_low)
            def _():
                low.wait_send()

            @pl.when(has_high)
            def _():
                high.wait_send()

    def stage(ex, part, i, rows):
        for c in range(2):
            zs[ex, 0, part, c, pl.ds(i, 1), :] = rows[c][0:1]
            zs[ex, 1, part, c, pl.ds(i, 1), :] = rows[c][nz - 1:nz]

    def slope_x(f):
        ahead = jnp.where(lane == nx - 1, 0.0, pltpu.roll(f, nx - 1, 1))
        behind = jnp.where(lane == 0, 0.0, pltpu.roll(f, 1, 1))
        return 0.5 * (ahead - behind)

    def slope_z(f, ex, c, part, i):
        below = jnp.broadcast_to(zr[ex, 0, part, c, pl.ds(i, 1), :], (nz, nx))
        above = jnp.broadcast_to(zr[ex, 1, part, c, pl.ds(i, 1), :], (nz, nx))
        ahead = jnp.where(sub == nz - 1, above, pltpu.roll(f, nz - 1, 0))
        behind = jnp.where(sub == 0, below, pltpu.roll(f, 1, 0))
        return 0.5 * (ahead - behind)

    def curl(field, ex, part, i):
        y = part * depth + i
        f = [field[c, y + 1] for c in range(3)]
        dy_x = 0.5 * (field[0, y + 2] - field[0, y])
        dy_z = 0.5 * (field[2, y + 2] - field[2, y])
        return (
            dy_z - slope_z(f[1], ex, 1, part, i),
            slope_z(f[0], ex, 0, part, i) - slope_x(f[2]),
            slope_x(f[1]) - dy_x,
        ), f

    def each_row(body, part, unroll=2):
        def some(step, carry):
            for u in range(unroll):
                body(part, step * unroll + u)
            return carry

        lax.fori_loop(0, depth // unroll, some, 0)

    loads[0].wait()
    for part in range(parts):
        each_row(lambda p, i: stage(0, p, i, (bE[0, p * depth + i + 1], bE[1, p * depth + i + 1])), part, 4)
    count = groups - 1 + has_low.astype(jnp.int32) + has_high.astype(jnp.int32)
    pl.semaphore_wait(barrier, count)
    send_z(0, 0)
    send_left(bE, 0)
    send_right(bE, 0)
    for part in range(1, parts):
        send_z(0, part)

    loads[1].wait()
    local_solve(wE, 1, 0)
    for copy in gather(0):
        copy.start()

    for load in loads[2:]:
        load.wait()

    def argument(part, i):
        y = part * depth + i
        spread = eta[y] * (1.0 - (1.0 - iron_factor) * iron[y].astype(jnp.float32))
        eta[y] = spread
        turn, b = curl(bE, 0, part, i)
        s = [v[c, y] for c in range(3)]
        rows = (
            s[1] * b[2] - s[2] * b[1] - spread * turn[0],
            s[2] * b[0] - s[0] * b[2] - spread * turn[1],
            s[0] * b[1] - s[1] * b[0] - spread * turn[2],
        )
        for c in range(3):
            gE[c, y + 1] = rows[c]
        stage(1, part, i, rows)

    recv_left(bE, 0)
    for part in range(parts):
        if part == parts - 1:
            recv_right(bE, 0)
        recv_z(0, part)
        each_row(argument, part)
        send_z(1, part)
        if part == 0:
            send_left(gE, 1)
    send_right(gE, 1)

    gather_wait(0)
    lefts, rights = interface(0, wE, 1)
    for c in range(3):
        wE[c, 0] = lefts[c]
        wE[c, n + 1] = rights[c]

    def relax(part, i):
        y = part * depth + i
        near, far = al_tab[y], al_tab[n - 1 - y]
        rows = [wE[c, y + 1] + near * wE[c, 0] + far * wE[c, n + 1] for c in range(3)]
        for c in range(3):
            wE[c, y + 1] = rows[c]
        stage(2, part, i, rows)

    for part in range(parts):
        each_row(relax, part)
        send_z(2, part)

    def advance(part, i):
        y = part * depth + i
        turn, _ = curl(gE, 1, part, i)
        for c in range(3):
            new[c, y] = bE[c, y + 1] + step_size * turn[c]

    recv_left(gE, 1)
    for part in range(parts):
        if part == parts - 1:
            recv_right(gE, 1)
        recv_z(1, part)
        each_row(advance, part)
    local_solve(new, 0, 1)
    for copy in gather(1):
        copy.start()

    def pull(part, i):
        y = part * depth + i
        turn, w = curl(wE, 2, part, i)
        s = [v[c, y] for c in range(3)]
        spread = eta[y]
        adj[0, y] = w[0] + step_size * (turn[1] * s[2] - turn[2] * s[1])
        adj[1, y] = w[1] + step_size * (turn[2] * s[0] - turn[0] * s[2])
        adj[2, y] = w[2] + step_size * (turn[0] * s[1] - turn[1] * s[0])
        rows = [spread * turn[c] for c in range(3)]
        for c in range(3):
            hE[c, y + 1] = rows[c]
        stage(3, part, i, rows)

    for part in range(parts):
        recv_z(2, part)
        each_row(pull, part)
        send_z(3, part)
        if part == 0:
            send_left(hE, 3)
    send_right(hE, 3)

    def finish_adjoint(part, i):
        y = part * depth + i
        turn, _ = curl(hE, 3, part, i)
        for c in range(3):
            adj[c, y] = adj[c, y] - step_size * turn[c]

    def finish(part, i):
        y = part * depth + i
        near, far = al_tab[y], al_tab[n - 1 - y]
        for c in range(3):
            new[c, y] = new[c, y] + near * gE[c, 0] + far * gE[c, n + 1]

    gather_wait(1)
    lefts, rights = interface(1, new, 0)
    for c in range(3):
        gE[c, 0] = lefts[c]
        gE[c, n + 1] = rights[c]
    for part in range(parts):
        each_row(finish, part)

    recv_left(hE, 3)
    for part in range(parts):
        if part == parts - 1:
            recv_right(hE, 3)
        recv_z(3, part)
        each_row(finish_adjoint, part)

    done_sending(bE, 0)
    done_sending(gE, 1)
    done_sending(None, 2)
    done_sending(hE, 3)
    for slot in range(2):
        for copy in gather(slot):
            copy.wait_send()


def hand_over(new, adj, new_out, adj_out, sem):
    copies = [
        pltpu.make_async_copy(new, new_out, sem.at[0]),
        pltpu.make_async_copy(adj, adj_out, sem.at[1]),
    ]
    for copy in copies:
        copy.start()
    for copy in copies:
        copy.wait()


def local(groups, layers, magnetic, velocity, diffusivity, material, plane_rate, cotangent):
    _, n, nz, nx = magnetic.shape
    depth = 8 if n % 8 == 0 else n
    block = (3, n, nz, nx)
    rimmed = (3, n + 2, nz, nx)
    f32 = jnp.float32
    anywhere = pl.BlockSpec(memory_space=pl.ANY)
    inside = pl.BlockSpec(memory_space=pltpu.VMEM)
    args = [
        pltpu.with_memory_space_constraint(array, pltpu.HBM)
        for array in (magnetic, velocity, diffusivity, material, plane_rate.reshape(1, nz), cotangent)
    ]
    new, adj = pl.pallas_call(
        functools.partial(kernel, groups, layers, n),
        out_shape=[jax.ShapeDtypeStruct(block, f32)] * 2,
        in_specs=[anywhere] * 6,
        out_specs=[inside] * 2,
        scratch_shapes=[
            pltpu.VMEM(rimmed, f32),
            pltpu.VMEM(rimmed, f32),
            pltpu.VMEM(rimmed, f32),
            pltpu.VMEM(rimmed, f32),
            pltpu.VMEM(block, f32),
            pltpu.VMEM((n, nz, nx), f32),
            pltpu.VMEM((n, nz, nx), jnp.int32),
            pltpu.VMEM((1, nz), f32),
            pltpu.VMEM((4, 2, n // depth, 2, depth, nx), f32),
            pltpu.VMEM((4, 2, n // depth, 2, depth, nx), f32),
            pltpu.VMEM((2, groups, 3, nz, nx), f32),
            pltpu.VMEM((2, 2, 3, nz, nx), f32),
            pltpu.VMEM((n, nz, nx), f32),
            pltpu.VMEM((n, nz, nx), f32),
            pltpu.VMEM((n, nz, nx), f32),
            pltpu.VMEM((groups, nz, nx), f32),
            pltpu.VMEM((groups, nz, nx), f32),
            pltpu.VMEM((8, nz, nx), f32),
            pltpu.SemaphoreType.DMA((6,)),
            pltpu.SemaphoreType.DMA((4, 2, 2)),
            pltpu.SemaphoreType.DMA((4, 2, 2)),
            pltpu.SemaphoreType.DMA((4, 2, n // depth)),
            pltpu.SemaphoreType.DMA((4, 2, n // depth)),
            pltpu.SemaphoreType.DMA((2, groups)),
            pltpu.SemaphoreType.DMA((2, groups)),
        ],
        compiler_params=pltpu.CompilerParams(
            collective_id=0, has_side_effects=True, vmem_limit_bytes=24 * 2**20
        ),
    )(*args)
    return tuple(pl.pallas_call(
        hand_over,
        out_shape=[jax.ShapeDtypeStruct(block, f32)] * 2,
        in_specs=[anywhere] * 2,
        out_specs=[anywhere] * 2,
        scratch_shapes=[pltpu.SemaphoreType.DMA((2,))],
        compiler_params=pltpu.CompilerParams(vmem_limit_bytes=2**20),
    )(new, adj))


def solution(mesh):
    in_specs = (
        P(None, "gy", "gz", None),
        P(None, "gy", "gz", None),
        P("gy", "gz", None),
        P("gy", "gz", None),
        P("gz"),
        P(None, "gy", "gz", None),
    )
    out_specs = (P(None, "gy", "gz", None), P(None, "gy", "gz", None))
    body = functools.partial(local, mesh.shape["gy"], mesh.shape["gz"])
    return jax.shard_map(body, mesh=mesh, in_specs=in_specs, out_specs=out_specs, check_vma=False)
```

```python
import functools
import jax
import jax.numpy as jnp
from jax import lax
from jax.experimental import pallas as pl
from jax.experimental.pallas import tpu as pltpu
from jax.sharding import PartitionSpec as P

step_size = 0.1
iron_factor = 0.2
MESH = pl.DeviceIdType.MESH
Y_PARTS = (0, 2)
Z_PARTS = (0, 1)


def kernel(
    groups, layers, n, mag, vel, dif, mat, rate, cot, new, adj,
    bE, gE, wE, hE, v, eta, iron, rate_row, zs, zr, ends, sums, m_tab, inv_tab, al_tab, s_tab, den_tab, mix,
    load_sem, ys_sem, yr_sem, zs_sem, zr_sem, gs_sem, gr_sem,
):
    me = lax.axis_index("gy")
    lay = lax.axis_index("gz")
    nx = bE.shape[-1]
    nz = bE.shape[-2]
    parts, depth = zs.shape[2], zs.shape[4]

    rate_load = pltpu.make_async_copy(rate, rate_row, load_sem.at[5])
    rate_load.start()
    loads = [
        pltpu.make_async_copy(mag, bE.at[:, pl.ds(1, n)], load_sem.at[0]),
        pltpu.make_async_copy(cot, wE.at[:, pl.ds(1, n)], load_sem.at[1]),
        pltpu.make_async_copy(vel, v, load_sem.at[2]),
        pltpu.make_async_copy(dif, eta, load_sem.at[3]),
        pltpu.make_async_copy(mat, iron, load_sem.at[4]),
    ]
    for load in loads:
        load.start()

    has_left, has_right = me > 0, me < groups - 1
    has_low, has_high = lay > 0, lay < layers - 1

    barrier = pltpu.get_barrier_semaphore()
    for k in range(1, groups):
        pl.semaphore_signal(
            barrier, inc=1, device_id={"gy": lax.rem(me + k, groups), "gz": lay}, device_id_type=MESH
        )

    @pl.when(has_low)
    def _():
        pl.semaphore_signal(barrier, inc=1, device_id={"gy": me, "gz": lay - 1}, device_id_type=MESH)

    @pl.when(has_high)
    def _():
        pl.semaphore_signal(barrier, inc=1, device_id={"gy": me, "gz": lay + 1}, device_id_type=MESH)

    rim = jnp.zeros((nz, nx), jnp.float32)
    for field in (bE, gE, hE):
        for part in Y_PARTS:
            @pl.when(jnp.logical_not(has_left))
            def _():
                field[part, 0] = rim

            @pl.when(jnp.logical_not(has_right))
            def _():
                field[part, n + 1] = rim

    @pl.when(jnp.logical_not(has_low))
    def _():
        zr[:, 0] = jnp.zeros(zr.shape[:1] + zr.shape[2:], jnp.float32)

    @pl.when(jnp.logical_not(has_high))
    def _():
        zr[:, 1] = jnp.zeros(zr.shape[:1] + zr.shape[2:], jnp.float32)

    sub = lax.broadcasted_iota(jnp.int32, (nz, nx), 0)
    lane = lax.broadcasted_iota(jnp.int32, (nz, 128), 1)
    square = (
        lax.broadcasted_iota(jnp.int32, (nz, nz), 0) == lax.broadcasted_iota(jnp.int32, (nz, nz), 1)
    )
    rate_load.wait()
    r = jnp.sum(jnp.where(square, jnp.broadcast_to(rate_row[...], (nz, nz)), 0.0), axis=1, keepdims=True)
    r = jnp.broadcast_to(r, (nz, nx))

    def pivot(k, p):
        inv = 1.0 / (r + p)
        m = r * inv
        m_tab[k] = m
        inv_tab[k] = inv
        return 1.0 + m * p

    lax.fori_loop(0, n, pivot, 1.0 + r)

    def response(k, above):
        here = m_tab[n - 1 - k] * above
        al_tab[k] = here
        return here

    cc = lax.fori_loop(0, n, response, jnp.ones((nz, nx), jnp.float32))
    aa = m_tab[n - 1]

    def reach(k, s):
        s_tab[k] = s
        den = cc / (1.0 - s * aa)
        den_tab[k] = den
        return aa + cc * s * den

    lax.fori_loop(0, groups, reach, jnp.zeros((nz, nx), jnp.float32))
    s_low, s_high = s_tab[me], s_tab[groups - 1 - me]
    left_gap, right_gap = 1.0 - s_low * aa, 1.0 - s_high * aa
    det = 1.0 / (left_gap * right_gap - s_low * s_high * cc * cc)
    mix[0] = right_gap * det
    mix[1] = s_low * cc * det
    mix[2] = left_gap * det
    mix[3] = s_high * cc * det
    mix[4] = den_tab[me] * s_low
    mix[5] = den_tab[groups - 1 - me] * s_high
    mix[6] = s_low
    mix[7] = s_high

    def local_solve(field, offset, slot):
        def down(k, held):
            m = m_tab[jnp.maximum(k - 1, 0)]
            rows = tuple(field[c, offset + k] + m * held[c] for c in range(3))
            for c in range(3):
                field[c, offset + k] = rows[c]
            return rows

        zero = jnp.zeros((nz, nx), jnp.float32)
        lax.fori_loop(0, n, down, (zero, zero, zero), unroll=True)

        def up(step, held):
            k = n - 1 - step
            m, inv = m_tab[k], inv_tab[k]
            rows = tuple(field[c, offset + k] * inv + m * held[c] for c in range(3))
            for c in range(3):
                field[c, offset + k] = rows[c]
            return rows

        lax.fori_loop(0, n, up, (zero, zero, zero), unroll=True)
        for c in range(3):
            first, last = field[c, offset], field[c, offset + n - 1]
            sums[slot, 0, c] = last + mix[4] * first
            sums[slot, 1, c] = first + mix[5] * last

    def gather(slot):
        copies = []
        for k in range(1, groups):
            partner = lax.rem(me + k, groups)
            copies.append(pltpu.make_async_remote_copy(
                src_ref=sums.at[slot, (partner < me).astype(jnp.int32)], dst_ref=ends.at[slot, me],
                send_sem=gs_sem.at[slot, k], recv_sem=gr_sem.at[slot, k],
                device_id={"gy": partner, "gz": lay}, device_id_type=MESH,
            ))
        return copies

    def gather_wait(slot):
        for k in range(1, groups):
            src = lax.rem(me + groups - k, groups)
            pltpu.make_async_remote_copy(
                src_ref=ends.at[slot, src], dst_ref=ends.at[slot, src],
                send_sem=gs_sem.at[slot, k], recv_sem=gr_sem.at[slot, k],
                device_id={"gy": src, "gz": lay}, device_id_type=MESH,
            ).wait_recv()

    def interface(slot, field, offset):
        zero = jnp.zeros((nz, nx), jnp.float32)

        def sweep(k, held):
            low, high = held
            den = den_tab[k]
            far = groups - 1 - k
            low = tuple(jnp.where(k < me, ends[slot, k, c] + den * low[c], low[c]) for c in range(3))
            high = tuple(jnp.where(far > me, ends[slot, far, c] + den * high[c], high[c]) for c in range(3))
            return low, high

        zeros = (zero, zero, zero)
        low, high = lax.fori_loop(0, groups - 1, sweep, (zeros, zeros), unroll=groups <= 8)
        lefts, rights = [], []
        for c in range(3):
            x = low[c] + mix[6] * field[c, offset]
            y = high[c] + mix[7] * field[c, offset + n - 1]
            lefts.append(mix[0] * x + mix[1] * y)
            rights.append(mix[2] * y + mix[3] * x)
        return lefts, rights

    def y_copies(field, ex):
        lefts, rights = [], []
        for i, part in enumerate(Y_PARTS):
            lefts.append(pltpu.make_async_remote_copy(
                src_ref=field.at[part, 1], dst_ref=field.at[part, n + 1],
                send_sem=ys_sem.at[ex, 0, i], recv_sem=yr_sem.at[ex, 0, i],
                device_id={"gy": jnp.maximum(me - 1, 0), "gz": lay}, device_id_type=MESH))
            rights.append(pltpu.make_async_remote_copy(
                src_ref=field.at[part, n], dst_ref=field.at[part, 0],
                send_sem=ys_sem.at[ex, 1, i], recv_sem=yr_sem.at[ex, 1, i],
                device_id={"gy": jnp.minimum(me + 1, groups - 1), "gz": lay}, device_id_type=MESH))
        return lefts, rights

    def z_copies(ex, part):
        low = pltpu.make_async_remote_copy(
            src_ref=zs.at[ex, 0, part], dst_ref=zr.at[ex, 1, part],
            send_sem=zs_sem.at[ex, 0, part], recv_sem=zr_sem.at[ex, 0, part],
            device_id={"gy": me, "gz": jnp.maximum(lay - 1, 0)}, device_id_type=MESH)
        high = pltpu.make_async_remote_copy(
            src_ref=zs.at[ex, 1, part], dst_ref=zr.at[ex, 0, part],
            send_sem=zs_sem.at[ex, 1, part], recv_sem=zr_sem.at[ex, 1, part],
            device_id={"gy": me, "gz": jnp.minimum(lay + 1, layers - 1)}, device_id_type=MESH)
        return low, high

    def send_left(field, ex):
        @pl.when(has_left)
        def _():
            for copy in y_copies(field, ex)[0]:
                copy.start()

    def send_right(field, ex):
        @pl.when(has_right)
        def _():
            for copy in y_copies(field, ex)[1]:
                copy.start()

    def send_z(ex, part):
        low, high = z_copies(ex, part)

        @pl.when(has_low)
        def _():
            low.start()

        @pl.when(has_high)
        def _():
            high.start()

    def recv_left(field, ex):
        @pl.when(has_left)
        def _():
            for copy in y_copies(field, ex)[1]:
                copy.wait_recv()

    def recv_right(field, ex):
        @pl.when(has_right)
        def _():
            for copy in y_copies(field, ex)[0]:
                copy.wait_recv()

    def recv_z(ex, part):
        low, high = z_copies(ex, part)

        @pl.when(has_high)
        def _():
            low.wait_recv()

        @pl.when(has_low)
        def _():
            high.wait_recv()

    def done_sending(field, ex):
        if field is not None:
            lefts, rights = y_copies(field, ex)

            @pl.when(has_left)
            def _():
                for copy in lefts:
                    copy.wait_send()

            @pl.when(has_right)
            def _():
                for copy in rights:
                    copy.wait_send()

        for part in range(parts):
            low, high = z_copies(ex, part)

            @pl.when(has_low)
            def _():
                low.wait_send()

            @pl.when(has_high)
            def _():
                high.wait_send()

    def stage(ex, part, i, rows):
        for c in range(2):
            zs[ex, 0, part, c, pl.ds(i, 1), :] = rows[c][0:1]
            zs[ex, 1, part, c, pl.ds(i, 1), :] = rows[c][nz - 1:nz]

    def slope_x(f):
        width = lane.shape[1]
        tiles = [f[:, at:at + width] for at in range(0, nx, width)]
        ahead = [pltpu.roll(tile, width - 1, 1) for tile in tiles] + [jnp.zeros_like(tiles[0])]
        behind = [jnp.zeros_like(tiles[0])] + [pltpu.roll(tile, 1, 1) for tile in tiles]
        return jnp.concatenate(
            [
                jnp.where(lane == width - 1, ahead[t + 1], ahead[t])
                - jnp.where(lane == 0, behind[t], behind[t + 1])
                for t in range(len(tiles))
            ],
            axis=1,
        )

    def slope_z(f, ex, c, part, i):
        below = jnp.broadcast_to(zr[ex, 0, part, c, pl.ds(i, 1), :], (nz, nx))
        above = jnp.broadcast_to(zr[ex, 1, part, c, pl.ds(i, 1), :], (nz, nx))
        ahead = jnp.where(sub == nz - 1, above, pltpu.roll(f, nz - 1, 0))
        behind = jnp.where(sub == 0, below, pltpu.roll(f, 1, 0))
        return ahead - behind

    def curl(field, ex, part, i):
        y = part * depth + i
        f = [field[c, y + 1] for c in range(3)]
        dy_x = field[0, y + 2] - field[0, y]
        dy_z = field[2, y + 2] - field[2, y]
        return (
            dy_z - slope_z(f[1], ex, 1, part, i),
            slope_z(f[0], ex, 0, part, i) - slope_x(f[2]),
            slope_x(f[1]) - dy_x,
        ), f

    def each_row(body, part, unroll=4):
        def some(step, carry):
            for u in range(unroll):
                body(part, step * unroll + u)
            return carry

        lax.fori_loop(0, depth // unroll, some, 0)

    loads[0].wait()
    for part in range(parts):
        each_row(lambda p, i: stage(0, p, i, (bE[0, p * depth + i + 1], bE[1, p * depth + i + 1])), part, 4)
    count = groups - 1 + has_low.astype(jnp.int32) + has_high.astype(jnp.int32)
    pl.semaphore_wait(barrier, count)
    send_z(0, 0)
    send_left(bE, 0)
    send_right(bE, 0)
    for part in range(1, parts):
        send_z(0, part)

    loads[1].wait()
    local_solve(wE, 1, 0)
    for copy in gather(0):
        copy.start()

    for load in loads[2:]:
        load.wait()

    def argument(part, i):
        y = part * depth + i
        spread = eta[y] * (0.5 - 0.5 * (1.0 - iron_factor) * iron[y].astype(jnp.float32))
        eta[y] = spread
        turn, b = curl(bE, 0, part, i)
        s = [v[c, y] for c in range(3)]
        rows = (
            s[1] * b[2] - s[2] * b[1] - spread * turn[0],
            s[2] * b[0] - s[0] * b[2] - spread * turn[1],
            s[0] * b[1] - s[1] * b[0] - spread * turn[2],
        )
        for c in range(3):
            gE[c, y + 1] = rows[c]
        stage(1, part, i, rows)

    recv_left(bE, 0)
    for part in range(parts):
        if part == parts - 1:
            recv_right(bE, 0)
        recv_z(0, part)
        each_row(argument, part)
        send_z(1, part)
        if part == 0:
            send_left(gE, 1)
    send_right(gE, 1)

    gather_wait(0)
    lefts, rights = interface(0, wE, 1)
    for c in range(3):
        wE[c, 0] = lefts[c]
        wE[c, n + 1] = rights[c]

    def relax(part, i):
        y = part * depth + i
        near, far = al_tab[y], al_tab[n - 1 - y]
        rows = [wE[c, y + 1] + near * wE[c, 0] + far * wE[c, n + 1] for c in range(3)]
        for c in range(3):
            wE[c, y + 1] = rows[c]
        stage(2, part, i, rows)

    for part in range(parts):
        each_row(relax, part)
        send_z(2, part)

    def advance(part, i):
        y = part * depth + i
        turn, _ = curl(gE, 1, part, i)
        for c in range(3):
            new[c, y] = bE[c, y + 1] + 0.5 * step_size * turn[c]

    recv_left(gE, 1)
    for part in range(parts):
        if part == parts - 1:
            recv_right(gE, 1)
        recv_z(1, part)
        each_row(advance, part)
    local_solve(new, 0, 1)
    for copy in gather(1):
        copy.start()

    def pull(part, i):
        y = part * depth + i
        turn, w = curl(wE, 2, part, i)
        s = [v[c, y] for c in range(3)]
        spread = eta[y]
        adj[0, y] = w[0] + 0.5 * step_size * (turn[1] * s[2] - turn[2] * s[1])
        adj[1, y] = w[1] + 0.5 * step_size * (turn[2] * s[0] - turn[0] * s[2])
        adj[2, y] = w[2] + 0.5 * step_size * (turn[0] * s[1] - turn[1] * s[0])
        rows = [spread * turn[c] for c in range(3)]
        for c in range(3):
            hE[c, y + 1] = rows[c]
        stage(3, part, i, rows)

    for part in range(parts):
        recv_z(2, part)
        each_row(pull, part)
        send_z(3, part)
        if part == 0:
            send_left(hE, 3)
    send_right(hE, 3)

    def finish_adjoint(part, i):
        y = part * depth + i
        turn, _ = curl(hE, 3, part, i)
        for c in range(3):
            adj[c, y] = adj[c, y] - 0.5 * step_size * turn[c]

    def finish(part, i):
        y = part * depth + i
        near, far = al_tab[y], al_tab[n - 1 - y]
        for c in range(3):
            new[c, y] = new[c, y] + near * gE[c, 0] + far * gE[c, n + 1]

    gather_wait(1)
    lefts, rights = interface(1, new, 0)
    for c in range(3):
        gE[c, 0] = lefts[c]
        gE[c, n + 1] = rights[c]
    for part in range(parts):
        each_row(finish, part)

    recv_left(hE, 3)
    for part in range(parts):
        if part == parts - 1:
            recv_right(hE, 3)
        recv_z(3, part)
        each_row(finish_adjoint, part)

    done_sending(bE, 0)
    done_sending(gE, 1)
    done_sending(None, 2)
    done_sending(hE, 3)
    for slot in range(2):
        for copy in gather(slot):
            copy.wait_send()


def hand_over(new, adj, new_out, adj_out, sem):
    copies = [
        pltpu.make_async_copy(new, new_out, sem.at[0]),
        pltpu.make_async_copy(adj, adj_out, sem.at[1]),
    ]
    for copy in copies:
        copy.start()
    for copy in copies:
        copy.wait()


def local(groups, layers, magnetic, velocity, diffusivity, material, plane_rate, cotangent):
    _, n, nz, nx = magnetic.shape
    depth = 8 if n % 8 == 0 else n
    block = (3, n, nz, nx)
    rimmed = (3, n + 2, nz, nx)
    f32 = jnp.float32
    anywhere = pl.BlockSpec(memory_space=pl.ANY)
    inside = pl.BlockSpec(memory_space=pltpu.VMEM)
    args = [
        pltpu.with_memory_space_constraint(array, pltpu.HBM)
        for array in (magnetic, velocity, diffusivity, material, plane_rate.reshape(1, nz), cotangent)
    ]
    new, adj = pl.pallas_call(
        functools.partial(kernel, groups, layers, n),
        out_shape=[jax.ShapeDtypeStruct(block, f32)] * 2,
        in_specs=[anywhere] * 6,
        out_specs=[inside] * 2,
        scratch_shapes=[
            pltpu.VMEM(rimmed, f32),
            pltpu.VMEM(rimmed, f32),
            pltpu.VMEM(rimmed, f32),
            pltpu.VMEM(rimmed, f32),
            pltpu.VMEM(block, f32),
            pltpu.VMEM((n, nz, nx), f32),
            pltpu.VMEM((n, nz, nx), jnp.int32),
            pltpu.VMEM((1, nz), f32),
            pltpu.VMEM((4, 2, n // depth, 2, depth, nx), f32),
            pltpu.VMEM((4, 2, n // depth, 2, depth, nx), f32),
            pltpu.VMEM((2, groups, 3, nz, nx), f32),
            pltpu.VMEM((2, 2, 3, nz, nx), f32),
            pltpu.VMEM((n, nz, nx), f32),
            pltpu.VMEM((n, nz, nx), f32),
            pltpu.VMEM((n, nz, nx), f32),
            pltpu.VMEM((groups, nz, nx), f32),
            pltpu.VMEM((groups, nz, nx), f32),
            pltpu.VMEM((8, nz, nx), f32),
            pltpu.SemaphoreType.DMA((6,)),
            pltpu.SemaphoreType.DMA((4, 2, 2)),
            pltpu.SemaphoreType.DMA((4, 2, 2)),
            pltpu.SemaphoreType.DMA((4, 2, n // depth)),
            pltpu.SemaphoreType.DMA((4, 2, n // depth)),
            pltpu.SemaphoreType.DMA((2, groups)),
            pltpu.SemaphoreType.DMA((2, groups)),
        ],
        compiler_params=pltpu.CompilerParams(
            collective_id=0, has_side_effects=True, vmem_limit_bytes=24 * 2**20
        ),
    )(*args)
    return tuple(pl.pallas_call(
        hand_over,
        out_shape=[jax.ShapeDtypeStruct(block, f32)] * 2,
        in_specs=[anywhere] * 2,
        out_specs=[anywhere] * 2,
        scratch_shapes=[pltpu.SemaphoreType.DMA((2,))],
        compiler_params=pltpu.CompilerParams(vmem_limit_bytes=2**20),
    )(new, adj))


def solution(mesh):
    in_specs = (
        P(None, "gy", "gz", None),
        P(None, "gy", "gz", None),
        P("gy", "gz", None),
        P("gy", "gz", None),
        P("gz"),
        P(None, "gy", "gz", None),
    )
    out_specs = (P(None, "gy", "gz", None), P(None, "gy", "gz", None))
    body = functools.partial(local, mesh.shape["gy"], mesh.shape["gz"])
    return jax.shard_map(body, mesh=mesh, in_specs=in_specs, out_specs=out_specs, check_vma=False)
```

```python
import functools
import jax
import jax.numpy as jnp
from jax import lax
from jax.experimental import pallas as pl
from jax.experimental.pallas import tpu as pltpu
from jax.sharding import PartitionSpec as P

step_size = 0.1
iron_factor = 0.2
MESH = pl.DeviceIdType.MESH
Y_PARTS = (0, 2)
Z_PARTS = (0, 1)


def kernel(
    groups, layers, n, mag, vel, dif, mat, rate, cot, new, adj,
    bE, gE, wE, hE, v, eta, iron, rate_row, zs, zr, ends, sums, m_tab, inv_tab, al_tab, s_tab, den_tab, mix,
    load_sem, ys_sem, yr_sem, zs_sem, zr_sem, gs_sem, gr_sem,
):
    me = lax.axis_index("gy")
    lay = lax.axis_index("gz")
    nx = bE.shape[-1]
    nz = bE.shape[-2]
    parts, depth = zs.shape[2], zs.shape[4]

    rate_load = pltpu.make_async_copy(rate, rate_row, load_sem.at[5])
    rate_load.start()
    loads = [
        pltpu.make_async_copy(mag, bE.at[:, pl.ds(1, n)], load_sem.at[0]),
        pltpu.make_async_copy(cot, wE.at[:, pl.ds(1, n)], load_sem.at[1]),
        pltpu.make_async_copy(vel, v, load_sem.at[2]),
        pltpu.make_async_copy(dif, eta, load_sem.at[3]),
        pltpu.make_async_copy(mat, iron, load_sem.at[4]),
    ]
    for load in loads:
        load.start()

    has_left, has_right = me > 0, me < groups - 1
    has_low, has_high = lay > 0, lay < layers - 1

    barrier = pltpu.get_barrier_semaphore()
    for k in range(1, groups):
        pl.semaphore_signal(
            barrier, inc=1, device_id={"gy": lax.rem(me + k, groups), "gz": lay}, device_id_type=MESH
        )

    @pl.when(has_low)
    def _():
        pl.semaphore_signal(barrier, inc=1, device_id={"gy": me, "gz": lay - 1}, device_id_type=MESH)

    @pl.when(has_high)
    def _():
        pl.semaphore_signal(barrier, inc=1, device_id={"gy": me, "gz": lay + 1}, device_id_type=MESH)

    rim = jnp.zeros((nz, nx), jnp.float32)
    for field in (bE, gE, hE):
        for part in Y_PARTS:
            @pl.when(jnp.logical_not(has_left))
            def _():
                field[part, 0] = rim

            @pl.when(jnp.logical_not(has_right))
            def _():
                field[part, n + 1] = rim

    @pl.when(jnp.logical_not(has_low))
    def _():
        zr[:, 0] = jnp.zeros(zr.shape[:1] + zr.shape[2:], jnp.float32)

    @pl.when(jnp.logical_not(has_high))
    def _():
        zr[:, 1] = jnp.zeros(zr.shape[:1] + zr.shape[2:], jnp.float32)

    sub = lax.broadcasted_iota(jnp.int32, (nz, nx), 0)
    lane = lax.broadcasted_iota(jnp.int32, (nz, 128), 1)
    square = (
        lax.broadcasted_iota(jnp.int32, (nz, nz), 0) == lax.broadcasted_iota(jnp.int32, (nz, nz), 1)
    )
    rate_load.wait()
    r = jnp.sum(jnp.where(square, jnp.broadcast_to(rate_row[...], (nz, nz)), 0.0), axis=1, keepdims=True)
    r = jnp.broadcast_to(r, (nz, nx))

    def pivot(k, p):
        inv = 1.0 / (r + p)
        m = r * inv
        m_tab[k] = m
        inv_tab[k] = inv
        return 1.0 + m * p

    lax.fori_loop(0, n, pivot, 1.0 + r)

    def response(k, above):
        here = m_tab[n - 1 - k] * above
        al_tab[k] = here
        return here

    cc = lax.fori_loop(0, n, response, jnp.ones((nz, nx), jnp.float32))
    aa = m_tab[n - 1]

    def reach(k, s):
        s_tab[k] = s
        den = cc / (1.0 - s * aa)
        den_tab[k] = den
        return aa + cc * s * den

    lax.fori_loop(0, groups, reach, jnp.zeros((nz, nx), jnp.float32))
    s_low, s_high = s_tab[me], s_tab[groups - 1 - me]
    left_gap, right_gap = 1.0 - s_low * aa, 1.0 - s_high * aa
    det = 1.0 / (left_gap * right_gap - s_low * s_high * cc * cc)
    mix[0] = right_gap * det
    mix[1] = s_low * cc * det
    mix[2] = left_gap * det
    mix[3] = s_high * cc * det
    mix[4] = den_tab[me] * s_low
    mix[5] = den_tab[groups - 1 - me] * s_high
    mix[6] = s_low
    mix[7] = s_high

    def local_solve(field, offset, slot):
        def down(k, held):
            m = m_tab[jnp.maximum(k - 1, 0)]
            rows = tuple(field[c, offset + k] + m * held[c] for c in range(3))
            for c in range(3):
                field[c, offset + k] = rows[c]
            return rows

        zero = jnp.zeros((nz, nx), jnp.float32)
        lax.fori_loop(0, n, down, (zero, zero, zero), unroll=True)
        local_rise(field, offset, slot)

    def local_rise(field, offset, slot):
        zero = jnp.zeros((nz, nx), jnp.float32)

        def up(step, held):
            k = n - 1 - step
            m, inv = m_tab[k], inv_tab[k]
            rows = tuple(field[c, offset + k] * inv + m * held[c] for c in range(3))
            for c in range(3):
                field[c, offset + k] = rows[c]
            return rows

        lax.fori_loop(0, n, up, (zero, zero, zero), unroll=True)
        for c in range(3):
            first, last = field[c, offset], field[c, offset + n - 1]
            sums[slot, 0, c] = last + mix[4] * first
            sums[slot, 1, c] = first + mix[5] * last

    def gather(slot):
        copies = []
        for k in range(1, groups):
            partner = lax.rem(me + k, groups)
            copies.append(pltpu.make_async_remote_copy(
                src_ref=sums.at[slot, (partner < me).astype(jnp.int32)], dst_ref=ends.at[slot, me],
                send_sem=gs_sem.at[slot, k], recv_sem=gr_sem.at[slot, k],
                device_id={"gy": partner, "gz": lay}, device_id_type=MESH,
            ))
        return copies

    def gather_wait(slot):
        for k in range(1, groups):
            src = lax.rem(me + groups - k, groups)
            pltpu.make_async_remote_copy(
                src_ref=ends.at[slot, src], dst_ref=ends.at[slot, src],
                send_sem=gs_sem.at[slot, k], recv_sem=gr_sem.at[slot, k],
                device_id={"gy": src, "gz": lay}, device_id_type=MESH,
            ).wait_recv()

    def interface(slot, field, offset):
        zero = jnp.zeros((nz, nx), jnp.float32)

        def sweep(k, held):
            low, high = held
            den = den_tab[k]
            far = groups - 1 - k
            low = tuple(jnp.where(k < me, ends[slot, k, c] + den * low[c], low[c]) for c in range(3))
            high = tuple(jnp.where(far > me, ends[slot, far, c] + den * high[c], high[c]) for c in range(3))
            return low, high

        zeros = (zero, zero, zero)
        low, high = lax.fori_loop(0, groups - 1, sweep, (zeros, zeros), unroll=groups <= 8)
        lefts, rights = [], []
        for c in range(3):
            x = low[c] + mix[6] * field[c, offset]
            y = high[c] + mix[7] * field[c, offset + n - 1]
            lefts.append(mix[0] * x + mix[1] * y)
            rights.append(mix[2] * y + mix[3] * x)
        return lefts, rights

    def y_copies(field, ex):
        lefts, rights = [], []
        for i, part in enumerate(Y_PARTS):
            lefts.append(pltpu.make_async_remote_copy(
                src_ref=field.at[part, 1], dst_ref=field.at[part, n + 1],
                send_sem=ys_sem.at[ex, 0, i], recv_sem=yr_sem.at[ex, 0, i],
                device_id={"gy": jnp.maximum(me - 1, 0), "gz": lay}, device_id_type=MESH))
            rights.append(pltpu.make_async_remote_copy(
                src_ref=field.at[part, n], dst_ref=field.at[part, 0],
                send_sem=ys_sem.at[ex, 1, i], recv_sem=yr_sem.at[ex, 1, i],
                device_id={"gy": jnp.minimum(me + 1, groups - 1), "gz": lay}, device_id_type=MESH))
        return lefts, rights

    def z_copies(ex, part):
        low = pltpu.make_async_remote_copy(
            src_ref=zs.at[ex, 0, part], dst_ref=zr.at[ex, 1, part],
            send_sem=zs_sem.at[ex, 0, part], recv_sem=zr_sem.at[ex, 0, part],
            device_id={"gy": me, "gz": jnp.maximum(lay - 1, 0)}, device_id_type=MESH)
        high = pltpu.make_async_remote_copy(
            src_ref=zs.at[ex, 1, part], dst_ref=zr.at[ex, 0, part],
            send_sem=zs_sem.at[ex, 1, part], recv_sem=zr_sem.at[ex, 1, part],
            device_id={"gy": me, "gz": jnp.minimum(lay + 1, layers - 1)}, device_id_type=MESH)
        return low, high

    def send_left(field, ex):
        @pl.when(has_left)
        def _():
            for copy in y_copies(field, ex)[0]:
                copy.start()

    def send_right(field, ex):
        @pl.when(has_right)
        def _():
            for copy in y_copies(field, ex)[1]:
                copy.start()

    def send_z(ex, part):
        low, high = z_copies(ex, part)

        @pl.when(has_low)
        def _():
            low.start()

        @pl.when(has_high)
        def _():
            high.start()

    def recv_left(field, ex):
        @pl.when(has_left)
        def _():
            for copy in y_copies(field, ex)[1]:
                copy.wait_recv()

    def recv_right(field, ex):
        @pl.when(has_right)
        def _():
            for copy in y_copies(field, ex)[0]:
                copy.wait_recv()

    def recv_z(ex, part):
        low, high = z_copies(ex, part)

        @pl.when(has_high)
        def _():
            low.wait_recv()

        @pl.when(has_low)
        def _():
            high.wait_recv()

    def done_sending(field, ex):
        if field is not None:
            lefts, rights = y_copies(field, ex)

            @pl.when(has_left)
            def _():
                for copy in lefts:
                    copy.wait_send()

            @pl.when(has_right)
            def _():
                for copy in rights:
                    copy.wait_send()

        for part in range(parts):
            low, high = z_copies(ex, part)

            @pl.when(has_low)
            def _():
                low.wait_send()

            @pl.when(has_high)
            def _():
                high.wait_send()

    def stage(ex, part, i, rows):
        for c in range(2):
            zs[ex, 0, part, c, pl.ds(i, 1), :] = rows[c][0:1]
            zs[ex, 1, part, c, pl.ds(i, 1), :] = rows[c][nz - 1:nz]

    def slope_x(f):
        width = lane.shape[1]
        tiles = [f[:, at:at + width] for at in range(0, nx, width)]
        ahead = [pltpu.roll(tile, width - 1, 1) for tile in tiles] + [jnp.zeros_like(tiles[0])]
        behind = [jnp.zeros_like(tiles[0])] + [pltpu.roll(tile, 1, 1) for tile in tiles]
        return jnp.concatenate(
            [
                jnp.where(lane == width - 1, ahead[t + 1], ahead[t])
                - jnp.where(lane == 0, behind[t], behind[t + 1])
                for t in range(len(tiles))
            ],
            axis=1,
        )

    def slope_z(f, ex, c, part, i):
        below = jnp.broadcast_to(zr[ex, 0, part, c, pl.ds(i, 1), :], (nz, nx))
        above = jnp.broadcast_to(zr[ex, 1, part, c, pl.ds(i, 1), :], (nz, nx))
        ahead = jnp.where(sub == nz - 1, above, pltpu.roll(f, nz - 1, 0))
        behind = jnp.where(sub == 0, below, pltpu.roll(f, 1, 0))
        return ahead - behind

    def curl(field, ex, part, i):
        y = part * depth + i
        f = [field[c, y + 1] for c in range(3)]
        dy_x = field[0, y + 2] - field[0, y]
        dy_z = field[2, y + 2] - field[2, y]
        return (
            dy_z - slope_z(f[1], ex, 1, part, i),
            slope_z(f[0], ex, 0, part, i) - slope_x(f[2]),
            slope_x(f[1]) - dy_x,
        ), f

    def each_row(body, part, unroll=4):
        def some(step, carry):
            for u in range(unroll):
                body(part, step * unroll + u)
            return carry

        lax.fori_loop(0, depth // unroll, some, 0)

    loads[0].wait()
    for part in range(parts):
        each_row(lambda p, i: stage(0, p, i, (bE[0, p * depth + i + 1], bE[1, p * depth + i + 1])), part, 4)
    count = groups - 1 + has_low.astype(jnp.int32) + has_high.astype(jnp.int32)
    pl.semaphore_wait(barrier, count)
    send_z(0, 0)
    send_left(bE, 0)
    send_right(bE, 0)
    for part in range(1, parts):
        send_z(0, part)

    loads[1].wait()
    local_solve(wE, 1, 0)
    for copy in gather(0):
        copy.start()

    for load in loads[2:]:
        load.wait()

    def argument(part, i):
        y = part * depth + i
        spread = eta[y] * (0.5 - 0.5 * (1.0 - iron_factor) * iron[y].astype(jnp.float32))
        eta[y] = spread
        turn, b = curl(bE, 0, part, i)
        s = [v[c, y] for c in range(3)]
        rows = (
            s[1] * b[2] - s[2] * b[1] - spread * turn[0],
            s[2] * b[0] - s[0] * b[2] - spread * turn[1],
            s[0] * b[1] - s[1] * b[0] - spread * turn[2],
        )
        for c in range(3):
            gE[c, y + 1] = rows[c]
        stage(1, part, i, rows)

    recv_left(bE, 0)
    for part in range(parts):
        if part == parts - 1:
            recv_right(bE, 0)
        recv_z(0, part)
        each_row(argument, part)
        send_z(1, part)
        if part == 0:
            send_left(gE, 1)
    send_right(gE, 1)

    gather_wait(0)
    lefts, rights = interface(0, wE, 1)
    for c in range(3):
        wE[c, 0] = lefts[c]
        wE[c, n + 1] = rights[c]

    def relax(part, i):
        y = part * depth + i
        near, far = al_tab[y], al_tab[n - 1 - y]
        rows = [wE[c, y + 1] + near * wE[c, 0] + far * wE[c, n + 1] for c in range(3)]
        for c in range(3):
            wE[c, y + 1] = rows[c]
        stage(2, part, i, rows)

    for part in range(parts):
        each_row(relax, part)
        send_z(2, part)

    def advance(part, i, above):
        y = part * depth + i
        turn, b = curl(gE, 1, part, i)
        m = m_tab[jnp.maximum(y - 1, 0)]
        rows = tuple(bE[c, y + 1] + 0.5 * step_size * turn[c] + m * above[c] for c in range(3))
        for c in range(3):
            new[c, y] = rows[c]
        return rows

    def advance_part(part, above):
        def some(step, held):
            for u in range(4):
                held = advance(part, step * 4 + u, held)
            return held

        return lax.fori_loop(0, depth // 4, some, above)

    recv_left(gE, 1)
    carried = (rim, rim, rim)
    for part in range(parts):
        if part == parts - 1:
            recv_right(gE, 1)
        recv_z(1, part)
        carried = advance_part(part, carried)
    local_rise(new, 0, 1)
    for copy in gather(1):
        copy.start()

    def pull(part, i):
        y = part * depth + i
        turn, w = curl(wE, 2, part, i)
        s = [v[c, y] for c in range(3)]
        spread = eta[y]
        adj[0, y] = w[0] + 0.5 * step_size * (turn[1] * s[2] - turn[2] * s[1])
        adj[1, y] = w[1] + 0.5 * step_size * (turn[2] * s[0] - turn[0] * s[2])
        adj[2, y] = w[2] + 0.5 * step_size * (turn[0] * s[1] - turn[1] * s[0])
        rows = [spread * turn[c] for c in range(3)]
        for c in range(3):
            hE[c, y + 1] = rows[c]
        stage(3, part, i, rows)

    for part in range(parts):
        recv_z(2, part)
        each_row(pull, part)
        send_z(3, part)
        if part == 0:
            send_left(hE, 3)
    send_right(hE, 3)

    def finish_adjoint(part, i):
        y = part * depth + i
        turn, _ = curl(hE, 3, part, i)
        for c in range(3):
            adj[c, y] = adj[c, y] - 0.5 * step_size * turn[c]

    def finish(part, i):
        y = part * depth + i
        near, far = al_tab[y], al_tab[n - 1 - y]
        for c in range(3):
            new[c, y] = new[c, y] + near * gE[c, 0] + far * gE[c, n + 1]

    gather_wait(1)
    lefts, rights = interface(1, new, 0)
    for c in range(3):
        gE[c, 0] = lefts[c]
        gE[c, n + 1] = rights[c]
    for part in range(parts):
        each_row(finish, part)

    recv_left(hE, 3)
    for part in range(parts):
        if part == parts - 1:
            recv_right(hE, 3)
        recv_z(3, part)
        each_row(finish_adjoint, part)

    done_sending(bE, 0)
    done_sending(gE, 1)
    done_sending(None, 2)
    done_sending(hE, 3)
    for slot in range(2):
        for copy in gather(slot):
            copy.wait_send()


def hand_over(new, adj, new_out, adj_out, sem):
    copies = [
        pltpu.make_async_copy(new, new_out, sem.at[0]),
        pltpu.make_async_copy(adj, adj_out, sem.at[1]),
    ]
    for copy in copies:
        copy.start()
    for copy in copies:
        copy.wait()


def local(groups, layers, magnetic, velocity, diffusivity, material, plane_rate, cotangent):
    _, n, nz, nx = magnetic.shape
    depth = 8 if n % 8 == 0 else n
    block = (3, n, nz, nx)
    rimmed = (3, n + 2, nz, nx)
    f32 = jnp.float32
    anywhere = pl.BlockSpec(memory_space=pl.ANY)
    inside = pl.BlockSpec(memory_space=pltpu.VMEM)
    args = [
        pltpu.with_memory_space_constraint(array, pltpu.HBM)
        for array in (magnetic, velocity, diffusivity, material, plane_rate.reshape(1, nz), cotangent)
    ]
    new, adj = pl.pallas_call(
        functools.partial(kernel, groups, layers, n),
        out_shape=[jax.ShapeDtypeStruct(block, f32)] * 2,
        in_specs=[anywhere] * 6,
        out_specs=[inside] * 2,
        scratch_shapes=[
            pltpu.VMEM(rimmed, f32),
            pltpu.VMEM(rimmed, f32),
            pltpu.VMEM(rimmed, f32),
            pltpu.VMEM(rimmed, f32),
            pltpu.VMEM(block, f32),
            pltpu.VMEM((n, nz, nx), f32),
            pltpu.VMEM((n, nz, nx), jnp.int32),
            pltpu.VMEM((1, nz), f32),
            pltpu.VMEM((4, 2, n // depth, 2, depth, nx), f32),
            pltpu.VMEM((4, 2, n // depth, 2, depth, nx), f32),
            pltpu.VMEM((2, groups, 3, nz, nx), f32),
            pltpu.VMEM((2, 2, 3, nz, nx), f32),
            pltpu.VMEM((n, nz, nx), f32),
            pltpu.VMEM((n, nz, nx), f32),
            pltpu.VMEM((n, nz, nx), f32),
            pltpu.VMEM((groups, nz, nx), f32),
            pltpu.VMEM((groups, nz, nx), f32),
            pltpu.VMEM((8, nz, nx), f32),
            pltpu.SemaphoreType.DMA((6,)),
            pltpu.SemaphoreType.DMA((4, 2, 2)),
            pltpu.SemaphoreType.DMA((4, 2, 2)),
            pltpu.SemaphoreType.DMA((4, 2, n // depth)),
            pltpu.SemaphoreType.DMA((4, 2, n // depth)),
            pltpu.SemaphoreType.DMA((2, groups)),
            pltpu.SemaphoreType.DMA((2, groups)),
        ],
        compiler_params=pltpu.CompilerParams(
            collective_id=0, has_side_effects=True, vmem_limit_bytes=24 * 2**20
        ),
    )(*args)
    return tuple(pl.pallas_call(
        hand_over,
        out_shape=[jax.ShapeDtypeStruct(block, f32)] * 2,
        in_specs=[anywhere] * 2,
        out_specs=[anywhere] * 2,
        scratch_shapes=[pltpu.SemaphoreType.DMA((2,))],
        compiler_params=pltpu.CompilerParams(vmem_limit_bytes=2**20),
    )(new, adj))


def solution(mesh):
    in_specs = (
        P(None, "gy", "gz", None),
        P(None, "gy", "gz", None),
        P("gy", "gz", None),
        P("gy", "gz", None),
        P("gz"),
        P(None, "gy", "gz", None),
    )
    out_specs = (P(None, "gy", "gz", None), P(None, "gy", "gz", None))
    body = functools.partial(local, mesh.shape["gy"], mesh.shape["gz"])
    return jax.shard_map(body, mesh=mesh, in_specs=in_specs, out_specs=out_specs, check_vma=False)
```
